128 devices in a mesh: wide: 32 (over x, z, y_lo), narrow: 4 (over y_hi, core).
Axes of the slice: x: 4, y: 4 (y_hi: 2, y_lo: 2; y = y_hi * 2 + y_lo), z: 4, core: 2. Of those that a mesh axis runs over, the one named last changes fastest.
Arguments:
- fine_in: bfloat16 [16, 64, 256, 512], P(None, None, 'wide', 'narrow'), may hold values from -6 to 6
- coarse_in: bfloat16 [64, 64, 64, 128], P(None, 'wide', 'narrow'), may hold values from -6 to 6
- w_fine1: bfloat16 [16, 16, 3, 3, 3], replicated, may hold values from -0.3125 to 0.3125
- b_fine1: float32 [16], replicated, may hold values from -3 to 3
- w_fine2: bfloat16 [16, 16, 3, 3, 3], replicated, may hold values from -0.3125 to 0.3125
- b_fine2: float32 [16], replicated, may hold values from -3 to 3
- w_coarse1: bfloat16 [64, 80, 3, 3, 3], replicated, may hold values from -0.125 to 0.125
- b_coarse1: float32 [64], replicated, may hold values from -3 to 3
- w_coarse2: bfloat16 [64, 64, 3, 3, 3], replicated, may hold values from -0.15625 to 0.15625
- b_coarse2: float32 [64], replicated, may hold values from -3 to 3
- w_proj: bfloat16 [16, 64], replicated, may hold values from -0.75 to 0.75
Outputs:
- fine_out: bfloat16 [16, 64, 256, 512], P(None, None, 'wide', 'narrow')
- coarse_out: bfloat16 [64, 64, 64, 128], P(None, 'wide', 'narrow')
The draws below stay inside these ranges and needn't reach their ends.
All inputs are finite; a program needn't handle non-finite values.
Results may differ from the reference program's by a relative error of at most 0.0075.
Values may be sent and summed in bfloat16 or wider, within the bound.
No kernel may reach another device: no remote copies, remote signals or barrier semaphores. Data moves between devices by JAX's collectives and lax.ppermute only.
A program may use at most 192 MiB of HBM per device.

```python
import jax
import jax.numpy as jnp
from jax import lax

CF = 16
CC = 64
Z = 64
FY = 256
FX = 512
CY = 64
CX = 128


def levels(own_key, dims, pieces, smallest, high):
    def one(dim, parts):
        draws = jax.random.uniform(jax.random.fold_in(jax.random.fold_in(own_key, 6), dim), (parts,), jnp.float32, smallest / len(pieces), high / len(pieces))
        return jnp.repeat(jnp.exp(draws), dims[dim] // parts).reshape((-1,) + (1,) * (len(dims) - dim - 1))

    loudness = one(*pieces[0])
    for cut in pieces[1:]:
        loudness = loudness * one(*cut)
    return loudness


def normal_values(rng, dims, width, bound, split=(), dtype=jnp.bfloat16):
    values = width * jax.random.normal(rng, dims, jnp.float32)
    if split:
        values = values * levels(rng, dims, split, -0.22, 0.18)
    return jnp.clip(values, -bound, bound).astype(dtype)


def setup_inputs(seed: int = 0) -> dict:
    streams_of = jax.random.split(jax.random.key(seed), 12)
    fine_in = normal_values(streams_of[0], (CF, Z, FY, FX), 1.0, 6.0, ((2, 32), (3, 4)))
    coarse_in = normal_values(streams_of[1], (CC, Z, CY, CX), 1.0, 6.0, ((1, 32), (2, 4)))
    w_fine1 = normal_values(streams_of[2], (CF, CF, 3, 3, 3), (CF * 27) ** -0.5, 0.3125)
    b_fine1 = normal_values(streams_of[3], (CF,), 0.5, 3.0, (), jnp.float32)
    w_fine2 = normal_values(streams_of[4], (CF, CF, 3, 3, 3), (CF * 27) ** -0.5, 0.3125)
    b_fine2 = normal_values(streams_of[5], (CF,), 0.5, 3.0, (), jnp.float32)
    w_coarse1 = normal_values(streams_of[6], (CC, CC + CF, 3, 3, 3), ((CC + CF) * 27) ** -0.5, 0.125)
    b_coarse1 = normal_values(streams_of[7], (CC,), 0.5, 3.0, (), jnp.float32)
    w_coarse2 = normal_values(streams_of[8], (CC, CC, 3, 3, 3), (CC * 27) ** -0.5, 0.15625)
    b_coarse2 = normal_values(streams_of[9], (CC,), 0.5, 3.0, (), jnp.float32)
    w_proj = normal_values(streams_of[10], (CF, CC), CC ** -0.5, 0.75)
    return {"fine_in": fine_in, "coarse_in": coarse_in, "w_fine1": w_fine1, "b_fine1": b_fine1, "w_fine2": w_fine2, "b_fine2": b_fine2, "w_coarse1": w_coarse1, "b_coarse1": b_coarse1, "w_coarse2": w_coarse2, "b_coarse2": b_coarse2, "w_proj": w_proj}


def convolve(field, kernel, offset):
    result = lax.conv_general_dilated(field.astype(jnp.float32)[None], kernel.astype(jnp.float32), (1, 1, 1), ((1, 1), (1, 1), (1, 1)), dimension_numbers=("NCDHW", "OIDHW", "NCDHW"), preferred_element_type=jnp.float32)[0]
    return result + offset[:, None, None, None]


def reference(fine_in, coarse_in, w_fine1, b_fine1, w_fine2, b_fine2, w_coarse1, b_coarse1, w_coarse2, b_coarse2, w_proj):
    hidden = jnp.maximum(convolve(fine_in, w_fine1, b_fine1), 0.0).astype(jnp.bfloat16)
    pooled = hidden.astype(jnp.float32).reshape(CF, Z, CY, 4, CX, 4).mean(axis=(3, 5)).astype(jnp.bfloat16)
    stacked = jnp.concatenate([coarse_in, pooled], axis=0)
    coarse_mid = jnp.maximum(convolve(stacked, w_coarse1, b_coarse1), 0.0).astype(jnp.bfloat16)
    coarse_out = jnp.maximum(convolve(coarse_mid, w_coarse2, b_coarse2), 0.0).astype(jnp.bfloat16)
    context = jnp.einsum("fc,czyx->fzyx", w_proj.astype(jnp.float32), coarse_out.astype(jnp.float32)).astype(jnp.bfloat16)
    fine_term = convolve(hidden, w_fine2, b_fine2)
    widened = jnp.broadcast_to(context[:, :, :, None, :, None], (CF, Z, CY, 4, CX, 4)).reshape(CF, Z, FY, FX)
    fine_out = (fine_term + widened.astype(jnp.float32)).astype(jnp.bfloat16)
    return fine_out, coarse_out
```

```python
import jax
import jax.numpy as jnp
from jax import lax
from jax.experimental import pallas as pl
from jax.experimental.pallas import tpu as pltpu
from jax.sharding import PartitionSpec as P

BF = jnp.bfloat16
F32 = jnp.float32
INTERPRET = False


def iota(shape, axis):
    return lax.broadcasted_iota(jnp.int32, shape, axis)


def onehot(mask):
    return jnp.where(mask, 1.0, 0.0).astype(BF)


def mm(a, b):
    return jnp.dot(a, b, preferred_element_type=F32)


def vm(n):
    return [pl.BlockSpec(memory_space=pltpu.VMEM)] * n


def outer_columns(rows, first_z):
    shape = (rows.shape[1], 128)
    r, lane = iota(shape, 0), iota(shape, 1)
    z, x = first_z + r // 128, r % 128
    return mm(rows, onehot(((x == 0) & (lane == z)) | ((x == 127) & (lane == z + 64))))


def prep_body(x_ref, t_ref, cols_ref, acc_ref):
    step = pl.program_id(0)
    zb = x_ref.shape[1]
    r, k = iota((128, 128), 0), iota((128, 128), 1)
    perm = onehot((r % 16) * 8 + r // 16 == k)
    rows = []
    for i in range(0, zb, 2):
        pair = jnp.concatenate([x_ref[:, i].reshape(128, 128), x_ref[:, i + 1].reshape(128, 128)], axis=1)
        out = mm(perm, pair).astype(BF)
        for j in range(2):
            t_ref[i + j] = out[:, j * 128 : j * 128 + 128]
        rows.append(out)
    part = outer_columns(jnp.concatenate(rows, axis=1), step * zb)

    @pl.when(step == 0)
    def _():
        acc_ref[...] = part

    @pl.when(step > 0)
    def _():
        acc_ref[...] += part

    cols_ref[...] = acc_ref[...].astype(BF)


def prep(x):
    zb = 8
    return pl.pallas_call(
        prep_body,
        grid=(64 // zb,),
        in_specs=[pl.BlockSpec((16, zb, 8, 128), lambda i: (0, i, 0, 0))],
        out_specs=[
            pl.BlockSpec((zb, 128, 128), lambda i: (i, 0, 0)),
            pl.BlockSpec((128, 128), lambda i: (0, 0)),
        ],
        out_shape=[jax.ShapeDtypeStruct((64, 128, 128), BF), jax.ShapeDtypeStruct((128, 128), BF)],
        scratch_shapes=[pltpu.VMEM((128, 128), F32)],
        interpret=INTERPRET,
        name="prep",
    )(x)


def cprep_body(x_ref, o_ref):
    r, k = iota((256, 256), 0), iota((256, 256), 1)
    perm = onehot((r % 16) * 16 + r // 16 == k)
    for g in range(4):
        pair = jnp.concatenate(
            [x_ref[g * 16 : g * 16 + 16, z].reshape(256, 128) for z in range(2)], axis=1
        )
        out = mm(perm, pair).astype(BF)
        for z in range(2):
            for y in range(16):
                o_ref[z, y, g * 16 : g * 16 + 16, :] = out[y * 16 : y * 16 + 16, z * 128 : z * 128 + 128]


def cprep(x):
    return pl.pallas_call(
        cprep_body,
        in_specs=vm(1),
        out_specs=vm(1)[0],
        out_shape=jax.ShapeDtypeStruct((2, 16, 64, 128), BF),
        interpret=INTERPRET,
        name="cprep",
    )(x)


def stage(z, x_ref, top_ref, bot_ref, tl_ref, tr_ref, s_ref):
    v = jnp.concatenate(
        [top_ref[pl.ds(pl.multiple_of(z * 16, 16), 16), :], x_ref[z], bot_ref[pl.ds(pl.multiple_of(z * 16, 16), 16), :]],
        axis=0,
    )
    f = v.astype(F32)
    lane = iota((160, 128), 1)
    left = jnp.where(lane == 0, pltpu.roll(tl_ref[...], lax.rem(192 - z, 128), 1), pltpu.roll(f, 1, 1))
    right = jnp.where(lane == 127, pltpu.roll(tr_ref[...], 127 - z, 1), pltpu.roll(f, 127, 1))
    base = pl.multiple_of((z + 1) * 512, 512)
    s_ref[pl.ds(base, 160), :] = left.astype(BF)
    s_ref[pl.ds(base + 160, 160), :] = v
    s_ref[pl.ds(base + 320, 160), :] = right.astype(BF)


def conv_pair(z, w_ref, s_ref):
    base = pl.multiple_of(z * 512, 512)
    rhs = jnp.concatenate([s_ref[pl.ds(base, 1536), :], s_ref[pl.ds(base + 512, 1536), :]], axis=1)
    return mm(w_ref[...], rhs)


def fine_setup(k_ref, top_ref, bot_ref, cl_ref, cr_ref, w_ref, w0_ref, s_ref, tl_ref, tr_ref, by_channel):
    w0_ref[...] = jnp.zeros((16, 1536), F32)
    for t in range(27):
        dz, dy, dx = t // 9, t // 3 % 3, t % 3
        at = dz * 512 + dx * 160 + dy * 16
        w0_ref[:, at : at + 16] = k_ref[t].astype(F32)
    w0 = w0_ref[...]
    for y in range(8):
        w_ref[y * 16 : y * 16 + 16, :] = (pltpu.roll(w0, y * 16, 1) if y else w0).astype(BF)
    if by_channel:
        r, k = iota((128, 128), 0), iota((128, 128), 1)
        w_ref[...] = mm(onehot((r % 8) * 16 + r // 8 == k), w_ref[...]).astype(BF)
    for ref, edge, col in ((tl_ref, 1024, cl_ref), (tr_ref, 1040, cr_ref)):
        ref[0:16, :] = top_ref[edge : edge + 16, :].astype(F32)
        ref[16:144, :] = col[...].astype(F32)
        ref[144:160, :] = bot_ref[edge : edge + 16, :].astype(F32)
    s_ref[0:512, :] = jnp.zeros((512, 128), BF)
    s_ref[65 * 512 : 66 * 512, :] = jnp.zeros((512, 128), BF)
    for z in range(1, 65):
        s_ref[z * 512 + 480 : z * 512 + 512, :] = jnp.zeros((32, 128), BF)


def run_conv(stage_fn, finish, w_ref, s_ref):
    for z in range(3):
        stage_fn(z)

    def step(i, _):
        out = conv_pair(2 * i, w_ref, s_ref)
        stage_fn(2 * i + 3)
        stage_fn(2 * i + 4)
        finish(i, out)
        return 0

    lax.fori_loop(0, 30, step, 0)
    out = conv_pair(60, w_ref, s_ref)
    stage_fn(63)
    finish(30, out)
    finish(31, conv_pair(62, w_ref, s_ref))


def fine1_body(x_ref, top_ref, bot_ref, cl_ref, cr_ref, k_ref, b_ref, h_ref, p_ref, cols_ref, s_ref, w_ref, w0_ref, tl_ref, tr_ref, acc_ref):
    fine_setup(k_ref, top_ref, bot_ref, cl_ref, cr_ref, w_ref, w0_ref, s_ref, tl_ref, tr_ref, False)
    bias = b_ref[...]

    def finish(i, out):
        h = jnp.maximum(out + bias, 0.0).astype(BF)
        parts = []
        for k in range(2):
            hz = h[:, k * 128 : (k + 1) * 128]
            h_ref[2 * i + k] = hz
            f = hz.astype(F32)
            for half in range(2):
                r = f[half * 64 : half * 64 + 64]
                parts.append((r[0:16] + r[16:32]) + (r[32:48] + r[48:64]))
        hi = [p.astype(BF) for p in parts]
        lo = [(p - q.astype(F32)).astype(BF) for p, q in zip(parts, hi)]
        acc_ref[pl.ds(pl.multiple_of(i * 16, 16), 16), :] = jnp.concatenate(hi + lo, axis=1)

    run_conv(lambda z: stage(z, x_ref, top_ref, bot_ref, tl_ref, tr_ref, s_ref), finish, w_ref, s_ref)
    r, lane = iota((1024, 128), 0) % 512, iota((1024, 128), 1)
    pick = jnp.where((r // 128) * 32 + (r % 128) // 4 == lane, 0.0625, 0.0).astype(BF)
    p_ref[...] = mm(acc_ref[...], pick).astype(BF)
    total = jnp.zeros((128, 128), F32)
    for g in range(8):
        total = total + outer_columns(jnp.concatenate([h_ref[g * 8 + k] for k in range(8)], axis=1), g * 8)
    cols_ref[...] = total.astype(BF)


def fine_scratch():
    return [
        pltpu.VMEM((66 * 512, 128), BF),
        pltpu.VMEM((128, 1536), BF),
        pltpu.VMEM((16, 1536), F32),
        pltpu.VMEM((160, 128), F32),
        pltpu.VMEM((160, 128), F32),
    ]


def fine1(x, top, bot, cl, cr, k, b):
    return pl.pallas_call(
        fine1_body,
        in_specs=vm(7),
        out_specs=vm(3),
        out_shape=[
            jax.ShapeDtypeStruct((64, 128, 128), BF),
            jax.ShapeDtypeStruct((512, 128), BF),
            jax.ShapeDtypeStruct((128, 128), BF),
        ],
        scratch_shapes=fine_scratch() + [pltpu.VMEM((512, 1024), BF)],
        interpret=INTERPRET,
        name="fine1",
    )(x, top, bot, cl, cr, k, b)


def fine2_body(x_ref, top_ref, bot_ref, cl_ref, cr_ref, k_ref, b_ref, o_ref, s_ref, w_ref, w0_ref, tl_ref, tr_ref):
    fine_setup(k_ref, top_ref, bot_ref, cl_ref, cr_ref, w_ref, w0_ref, s_ref, tl_ref, tr_ref, True)
    bias = b_ref[...]

    def finish(i, out):
        v = out + bias
        for k in range(2):
            o_ref[2 * i + k] = v[:, k * 128 : (k + 1) * 128]

    run_conv(lambda z: stage(z, x_ref, top_ref, bot_ref, tl_ref, tr_ref, s_ref), finish, w_ref, s_ref)


def fine2(x, top, bot, cl, cr, k, b):
    return pl.pallas_call(
        fine2_body,
        in_specs=vm(7),
        out_specs=vm(1)[0],
        out_shape=jax.ShapeDtypeStruct((64, 128, 128), F32),
        scratch_shapes=fine_scratch(),
        interpret=INTERPRET,
        name="fine2",
    )(x, top, bot, cl, cr, k, b)


def final_body(at_ref, t_ref, c_ref, o_ref):
    r, lane = iota((128, 512), 0), iota((128, 512), 1)
    up = onehot((lane // 128) * 32 + (lane % 128) // 4 == r)
    e = mm(c_ref[...].reshape(64, 128), up).astype(BF)
    rr, kk = iota((128, 32), 0), iota((128, 32), 1)
    spread = onehot((kk % 16 == rr // 8) & (kk // 16 == (rr % 8) // 4))
    for p in range(4):
        row = e[p * 16 : p * 16 + 16]
        both = [
            jnp.concatenate([row[:, k * 256 : k * 256 + 128], row[:, k * 256 + 128 : k * 256 + 256]], axis=0)
            for k in range(2)
        ]
        c = mm(spread, jnp.concatenate(both, axis=1))
        for k in range(2):
            v = t_ref[2 * p + k] + c[:, k * 128 : k * 128 + 128]
            o_ref[:, 2 * p + k] = v.reshape(16, 8, 128).astype(BF)


def final(at, t, c):
    return pl.pallas_call(
        final_body,
        grid_spec=pltpu.PrefetchScalarGridSpec(
            num_scalar_prefetch=1,
            grid=(8,),
            in_specs=[
                pl.BlockSpec((8, 128, 128), lambda i, at: (i, 0, 0)),
                pl.BlockSpec((4, 1, 16, 128), lambda i, at: (i, at[0], 0, 0)),
            ],
            out_specs=pl.BlockSpec((16, 8, 8, 128), lambda i, at: (0, i, 0, 0)),
        ),
        out_shape=jax.ShapeDtypeStruct((16, 64, 8, 128), BF),
        interpret=INTERPRET,
        name="final",
    )(at, t, c)


def spread_x(v):
    f = v.astype(F32)
    lane = iota(v.shape, 1)
    left = jnp.where(lane == 0, 0.0, pltpu.roll(f, 1, 1)).astype(BF)
    right = jnp.where(lane == 127, 0.0, pltpu.roll(f, 127, 1)).astype(BF)
    return jnp.concatenate([left, v, right], axis=0)


def window(s_ref, z, y, rows, per_z):
    both = []
    for k in range(2):
        parts = [
            s_ref[pl.ds(pl.multiple_of((z + dz) * per_z + (y + k) * rows, 16), 3 * rows), :] for dz in range(3)
        ]
        both.append(jnp.concatenate(parts, axis=0))
    return jnp.concatenate(both, axis=1)


def conv1a_body(par_ref, own_ref, mate_ref, far_ref, k_ref, b_ref, o_ref, s_ref, w_ref):
    even = par_ref[0] == 0
    for t in range(27):
        w_ref[:, t * 64 : t * 64 + 64] = k_ref[t][:, 0:64]

    def fill(y, _):
        for zi in range(6):
            if zi < 2:
                v = jnp.where(even, far_ref[zi, y], mate_ref[zi, y])
            elif zi < 4:
                v = own_ref[zi - 2, y]
            else:
                v = jnp.where(even, mate_ref[zi - 4, y], far_ref[zi - 4, y])
            s_ref[pl.ds(pl.multiple_of(zi * 3840 + y * 192, 64), 192), :] = spread_x(v)
        return 0

    lax.fori_loop(0, 20, fill, 0)
    bias = b_ref[...]

    def step(i, _):
        zo, yp = i // 9, lax.rem(i, 9)
        o_ref[i] = mm(w_ref[...], window(s_ref, zo, 2 * yp, 192, 3840)) + bias
        return 0

    lax.fori_loop(0, 36, step, 0)


def conv1a(par, own, mate, far, k, b):
    return pl.pallas_call(
        conv1a_body,
        in_specs=[pl.BlockSpec(memory_space=pltpu.SMEM)] + vm(5),
        out_specs=vm(1)[0],
        out_shape=jax.ShapeDtypeStruct((36, 64, 256), F32),
        scratch_shapes=[pltpu.VMEM((6 * 20 * 192, 128), BF), pltpu.VMEM((64, 1728), BF)],
        interpret=INTERPRET,
        name="conv1a",
    )(par, own, mate, far, k, b)


def coarse_body(at_ref, main_ref, lo_ref, hi_ref, part_ref, k1_ref, k2_ref, b_ref, proj_ref, out_ref, ctx_ref, sp_ref, sm_ref, w1_ref, w2_ref, co_ref, ct_ref):
    n, w = at_ref[0], at_ref[1]
    for t in range(27):
        w1_ref[:, t * 16 : t * 16 + 16] = k1_ref[t][:, 64:80]
        w2_ref[:, t * 64 : t * 64 + 64] = k2_ref[t]
    r, c = iota((512, 512), 0), iota((512, 512), 1)
    order = onehot((r % 128 // 32 == c // 128) & (r // 128 == c % 128 // 32) & (r % 32 == c % 32))
    for wb in range(10):
        if wb == 0:
            blocks = [jnp.where(n > 0, lo_ref[0, k], jnp.zeros((48, 128), BF)) for k in range(4)]
        elif wb == 9:
            blocks = [jnp.where(n < 3, hi_ref[0, k], jnp.zeros((48, 128), BF)) for k in range(4)]
        else:
            blocks = [main_ref[wb - 1, k] for k in range(4)]
        t = mm(jnp.concatenate(blocks, axis=1), order).astype(BF)
        for s in range(3):
            for zi in range(4):
                v = t[s * 16 : s * 16 + 16, zi * 128 : zi * 128 + 128]
                base = (2 * s + zi // 2) * 960 + (2 * wb + zi % 2) * 48
                sp_ref[base : base + 48, :] = spread_x(v)

    def mid(i, _):
        zo, yp = i // 9, lax.rem(i, 9)
        v = mm(w1_ref[...], window(sp_ref, zo, 2 * yp, 48, 960)) + part_ref[i]
        inside = ((zo > 0) | (w > 0)) & ((zo < 3) | (w < 31))
        first = inside & ((yp > 0) | (n > 0))
        second = inside & ((yp < 8) | (n < 3))
        v = jnp.maximum(v, 0.0)
        for k, keep in ((0, first), (1, second)):
            m = jnp.where(keep, v[:, k * 128 : k * 128 + 128], 0.0).astype(BF)
            sm_ref[pl.ds(pl.multiple_of(zo * 3456 + (2 * yp + k) * 192, 64), 192), :] = spread_x(m)
        return 0

    lax.fori_loop(0, 36, mid, 0)
    bias = b_ref[...]
    proj = proj_ref[...]
    for z in range(2):

        def last(b, _):
            o = jnp.maximum(mm(w2_ref[...], window(sm_ref, z, 2 * b, 192, 3456)) + bias, 0.0).astype(BF)
            ct = mm(proj, o).astype(BF)
            for k in range(2):
                lanes = slice(k * 128, k * 128 + 128)
                co_ref[pl.ds(pl.multiple_of((2 * b + k) * 64, 64), 64), z * 128 : z * 128 + 128] = o[:, lanes]
                at = (z * 2 + k) * 128
                ct_ref[pl.ds(pl.multiple_of(b * 16, 16), 16), at : at + 128] = ct[:, lanes]
            return 0

        lax.fori_loop(0, 8, last, 0)
    back = onehot((c % 128 // 32 == r // 128) & (c // 128 == r % 128 // 32) & (r % 32 == c % 32))
    ct = mm(ct_ref[...], back).astype(BF)
    for b in range(8):
        for k in range(4):
            ctx_ref[b, k] = ct[b * 16 : b * 16 + 16, k * 128 : k * 128 + 128]
    r, k = iota((256, 256), 0), iota((256, 256), 1)
    perm = onehot((r % 16) * 16 + r // 16 == k)
    for g in range(4):
        rows = jnp.concatenate([co_ref[y * 64 + g * 16 : y * 64 + g * 16 + 16, :] for y in range(16)], axis=0)
        o = mm(perm, rows).astype(BF)
        for z in range(2):
            out_ref[g * 16 : g * 16 + 16, z] = o[:, z * 128 : z * 128 + 128].reshape(16, 16, 128)


def coarse(at, got, part, k1, k2, b2, proj):
    def whole(shape):
        return pl.BlockSpec(shape, lambda i, at: (0,) * len(shape))

    return pl.pallas_call(
        coarse_body,
        grid_spec=pltpu.PrefetchScalarGridSpec(
            num_scalar_prefetch=1,
            grid=(1,),
            in_specs=[
                pl.BlockSpec((8, 4, 48, 128), lambda i, at: (at[0], 0, 0, 0)),
                pl.BlockSpec((1, 4, 48, 128), lambda i, at: (jnp.maximum(8 * at[0] - 1, 0), 0, 0, 0)),
                pl.BlockSpec((1, 4, 48, 128), lambda i, at: (jnp.minimum(8 * at[0] + 8, 31), 0, 0, 0)),
                whole((36, 64, 256)),
                whole((27, 64, 80)),
                whole((27, 64, 64)),
                whole((64, 1)),
                whole((16, 64)),
            ],
            out_specs=[whole((64, 2, 16, 128)), whole((8, 4, 16, 128))],
            scratch_shapes=[
                pltpu.VMEM((6 * 20 * 48, 128), BF),
                pltpu.VMEM((4 * 18 * 192, 128), BF),
                pltpu.VMEM((64, 432), BF),
                pltpu.VMEM((64, 1728), BF),
                pltpu.VMEM((1024, 256), BF),
                pltpu.VMEM((128, 512), BF),
            ],
        ),
        out_shape=[
            jax.ShapeDtypeStruct((64, 2, 16, 128), BF),
            jax.ShapeDtypeStruct((8, 4, 16, 128), BF),
        ],
        interpret=INTERPRET,
        name="coarse",
    )(at, got, got, got, part, k1, k2, b2, proj)


def shift(array, axis, by):
    count = lax.axis_size(axis)
    return lax.ppermute(array, axis, [(i, i + by) for i in range(count) if 0 <= i + by < count])


def across_y(rows, from_left, from_right):
    down = jnp.concatenate([rows[:, 112:128, :].reshape(1024, 128), from_left[112:128], from_right[112:128]], axis=0)
    up = jnp.concatenate([rows[:, 0:16, :].reshape(1024, 128), from_left[0:16], from_right[0:16]], axis=0)
    return shift(down, "wide", 1), shift(up, "wide", -1)


def taps(w):
    return jnp.transpose(w, (2, 3, 4, 0, 1)).reshape(27, w.shape[0], w.shape[1])


def local(
    fine_in,
    coarse_in,
    w_fine1,
    b_fine1,
    w_fine2,
    b_fine2,
    w_coarse1,
    b_coarse1,
    w_coarse2,
    b_coarse2,
    w_proj,
):
    w = lax.axis_index("wide")
    n = lax.axis_index("narrow")
    a, b = w // 8, w % 8
    rows, cols = prep(fine_in)
    ct = cprep(coarse_in)
    east = jnp.concatenate([cols, ct[:, 14:16].reshape(256, 128)], axis=0)
    west = jnp.concatenate([cols, ct[:, 0:2].reshape(256, 128)], axis=0)
    from_left = shift(east, "narrow", 1)
    from_right = shift(west, "narrow", -1)
    top, bottom = across_y(rows, from_left[0:128], from_right[0:128])
    slab = jnp.concatenate(
        [from_left[128:].reshape(2, 2, 64, 128), ct, from_right[128:].reshape(2, 2, 64, 128)], axis=1
    )
    mate = lax.ppermute(slab, "wide", [(i, i ^ 1) for i in range(32)])
    far = lax.ppermute(
        mate, "wide", [(i, i + 2 - 4 * (i % 2)) for i in range(32) if 0 <= i + 2 - 4 * (i % 2) < 32]
    )
    hidden, pooled, hcols = fine1(
        rows, top, bottom, from_left[0:128], from_right[0:128], taps(w_fine1), jnp.tile(b_fine1, 8)[:, None]
    )
    pooled = pooled.reshape(32, 16, 128)
    none = jnp.zeros((1, 16, 128), BF)
    three = jnp.stack(
        [jnp.concatenate([none, pooled[:-1]]), pooled, jnp.concatenate([pooled[1:], none])], axis=1
    ).reshape(32, 1, 48, 128)
    to = jnp.arange(4)
    goes = (to == a) | ((to == a + 1) & (b == 7)) | ((to == a - 1) & (b == 0))
    parcels = jnp.where(goes[None, :, None, None], three, jnp.zeros((), BF)).reshape(128, 48, 128)
    got = lax.all_to_all(parcels, ("wide", "narrow"), 0, 0, tiled=True).reshape(32, 4, 48, 128)
    part = conv1a((w % 2)[None], slab, mate, far, taps(w_coarse1), b_coarse1[:, None])
    hleft = shift(hcols, "narrow", 1)
    hright = shift(hcols, "narrow", -1)
    htop, hbottom = across_y(hidden, hleft, hright)
    coarse_out, context = coarse(
        jnp.stack([n, w]), got, part, taps(w_coarse1), taps(w_coarse2), b_coarse2[:, None], w_proj
    )
    back = jnp.where((to == n)[:, None, None, None, None], context[None], jnp.zeros((), BF)).reshape(128, 16, 128)
    arrived = lax.all_to_all(back, ("wide", "narrow"), 0, 0, tiled=True).reshape(32, 4, 16, 128)
    term = fine2(hidden, htop, hbottom, hleft, hright, taps(w_fine2), jnp.repeat(b_fine2, 8)[:, None])
    fine_out = final(a[None], term, arrived)
    return fine_out, coarse_out


def solution(mesh):
    f = jax.shard_map(
        local,
        mesh=mesh,
        in_specs=(P(None, None, "wide", "narrow"), P(None, "wide", "narrow", None)) + (P(),) * 9,
        out_specs=(P(None, None, "wide", "narrow"), P(None, "wide", "narrow", None)),
        check_vma=False,
    )
    return f
```

```python
import functools

import jax
import jax.numpy as jnp
from jax import lax
from jax.experimental import pallas as pl
from jax.experimental.pallas import tpu as pltpu
from jax.sharding import PartitionSpec as P


BF = jnp.bfloat16
F32 = jnp.float32
INTERPRET = False


def iota(shape, axis):
    return lax.broadcasted_iota(jnp.int32, shape, axis)


def onehot(mask):
    return jnp.where(mask, 1.0, 0.0).astype(BF)


def mm(a, b):
    return jnp.dot(a, b, preferred_element_type=F32)


def vm(n):
    return [pl.BlockSpec(memory_space=pltpu.VMEM)] * n


def outer_columns(rows, first_z):
    shape = (rows.shape[1], 128)
    r, lane = iota(shape, 0), iota(shape, 1)
    z, x = first_z + r // 128, r % 128
    return mm(rows, onehot(((x == 0) & (lane == z)) | ((x == 127) & (lane == z + 64))))


def prep_body(x_ref, t_ref, cols_ref, acc_ref):
    step = pl.program_id(0)
    zb = t_ref.shape[0]
    r, k = iota((128, 128), 0), iota((128, 128), 1)
    perm = onehot((r % 16) * 8 + r // 16 == k)
    rows = []
    for i in range(0, zb, 2):
        pair = jnp.concatenate([x_ref[:, step * zb + i + j].reshape(128, 128) for j in range(2)], axis=1)
        out = mm(perm, pair).astype(BF)
        for j in range(2):
            t_ref[i + j] = out[:, j * 128 : j * 128 + 128]
        rows.append(out)
    part = outer_columns(jnp.concatenate(rows, axis=1), step * zb)

    @pl.when(step == 0)
    def _():
        acc_ref[...] = part

    @pl.when(step > 0)
    def _():
        acc_ref[...] += part

    cols_ref[...] = acc_ref[...].astype(BF)


def prep(x):
    zb = 8
    return pl.pallas_call(
        prep_body,
        grid=(64 // zb,),
        in_specs=[pl.BlockSpec((16, 64, 8, 128), lambda i: (0, 0, 0, 0))],
        out_specs=[
            pl.BlockSpec((zb, 128, 128), lambda i: (i, 0, 0)),
            pl.BlockSpec((128, 128), lambda i: (0, 0)),
        ],
        out_shape=[jax.ShapeDtypeStruct((64, 128, 128), BF), jax.ShapeDtypeStruct((128, 128), BF)],
        scratch_shapes=[pltpu.VMEM((128, 128), F32)],
        interpret=INTERPRET,
        name="prep",
    )(x)


def cprep_body(x_ref, o_ref):
    r, k = iota((256, 256), 0), iota((256, 256), 1)
    perm = onehot((r % 16) * 16 + r // 16 == k)
    for g in range(4):
        pair = jnp.concatenate(
            [x_ref[g * 16 : g * 16 + 16, z].reshape(256, 128) for z in range(2)], axis=1
        )
        out = mm(perm, pair).astype(BF)
        for z in range(2):
            for y in range(16):
                o_ref[z, y, g * 16 : g * 16 + 16, :] = out[y * 16 : y * 16 + 16, z * 128 : z * 128 + 128]


def cprep(x):
    return pl.pallas_call(
        cprep_body,
        in_specs=vm(1),
        out_specs=vm(1)[0],
        out_shape=jax.ShapeDtypeStruct((2, 16, 64, 128), BF),
        interpret=INTERPRET,
        name="cprep",
    )(x)


def kept(ok, v):
    return jnp.where(ok, v, jnp.zeros((), BF))


def stage(z, at_ref, x_ref, top_ref, bot_ref, tl_ref, tr_ref, s_ref):
    rows = pl.ds(pl.multiple_of(z * 16, 16), 16)
    top = kept(at_ref[3] > 0, top_ref[rows, :])
    bot = kept(at_ref[3] < 31, bot_ref[rows, :])
    v = jnp.concatenate([top, x_ref[z], bot], axis=0)
    lane = iota((160, 128), 1)
    left = jnp.where(lane == 0, pltpu.roll(tl_ref[...], lax.rem(192 - z, 128), 1), pltpu.roll(v, 1, 1))
    right = jnp.where(lane == 127, pltpu.roll(tr_ref[...], 127 - z, 1), pltpu.roll(v, 127, 1))
    base = pl.multiple_of((z + 1) * 512, 512)
    s_ref[pl.ds(base, 160), :] = left
    s_ref[pl.ds(base + 160, 160), :] = v
    s_ref[pl.ds(base + 320, 160), :] = right


def conv_pair(z, w_ref, s_ref):
    base = pl.multiple_of(z * 512, 512)
    rhs = jnp.concatenate([s_ref[pl.ds(base, 1536), :], s_ref[pl.ds(base + 512, 1536), :]], axis=1)
    return mm(w_ref[...], rhs)


def bias_rows(b_ref, by_channel):
    r, k = iota((128, 16), 0), iota((128, 16), 1)
    mask = (r // 8 if by_channel else r % 16) == k
    return jnp.sum(jnp.where(mask, b_ref[...], 0.0), axis=1, keepdims=True)


def fine_setup(at_ref, k_ref, top_ref, bot_ref, cl_ref, cr_ref, w_ref, w0_ref, s_ref, tl_ref, tr_ref, by_channel):
    w0_ref[...] = jnp.zeros((16, 1536), F32)
    for t in range(27):
        dz, dy, dx = t // 9, t // 3 % 3, t % 3
        at = dz * 512 + dx * 160 + dy * 16
        w0_ref[:, at : at + 16] = k_ref[t].astype(F32)
    w0 = w0_ref[...]
    for y in range(8):
        w_ref[y * 16 : y * 16 + 16, :] = (pltpu.roll(w0, y * 16, 1) if y else w0).astype(BF)
    if by_channel:
        r, k = iota((128, 128), 0), iota((128, 128), 1)
        w_ref[...] = mm(onehot((r % 8) * 16 + r // 8 == k), w_ref[...]).astype(BF)
    n, w = at_ref[2], at_ref[3]
    for ref, edge, col, ok in ((tl_ref, 1024, cl_ref, n > 0), (tr_ref, 1040, cr_ref, n < 3)):
        ref[0:16, :] = kept(ok & (w > 0), top_ref[edge : edge + 16, :])
        ref[16:144, :] = kept(ok, col[0:128, :])
        ref[144:160, :] = kept(ok & (w < 31), bot_ref[edge : edge + 16, :])
    s_ref[0:512, :] = jnp.zeros((512, 128), BF)
    s_ref[65 * 512 : 66 * 512, :] = jnp.zeros((512, 128), BF)
    if not by_channel:
        for z in range(1, 65):
            s_ref[z * 512 + 480 : z * 512 + 512, :] = jnp.zeros((32, 128), BF)


def run_conv(stage_fn, finish, w_ref, s_ref):
    for z in range(5):
        stage_fn(z)

    def step(i, _):
        first = conv_pair(4 * i, w_ref, s_ref)
        second = conv_pair(4 * i + 2, w_ref, s_ref)
        for k in range(5, 9):
            stage_fn(4 * i + k)
        finish(2 * i, first)
        finish(2 * i + 1, second)
        return 0

    lax.fori_loop(0, 14, step, 0)
    first = conv_pair(56, w_ref, s_ref)
    second = conv_pair(58, w_ref, s_ref)
    for k in range(61, 64):
        stage_fn(k)
    finish(28, first)
    finish(29, second)
    first = conv_pair(60, w_ref, s_ref)
    second = conv_pair(62, w_ref, s_ref)
    finish(30, first)
    finish(31, second)


def fine1_body(at_ref, x_ref, top_ref, bot_ref, cl_ref, cr_ref, k_ref, b_ref, h_ref, p_ref, cols_ref, s_ref, w_ref, w0_ref, tl_ref, tr_ref, acc_ref):
    fine_setup(at_ref, k_ref, top_ref, bot_ref, cl_ref, cr_ref, w_ref, w0_ref, s_ref, tl_ref, tr_ref, False)
    bias = bias_rows(b_ref, False)

    def finish(i, out):
        h = jnp.maximum(out + bias, 0.0).astype(BF)
        parts = []
        for k in range(2):
            hz = h[:, k * 128 : (k + 1) * 128]
            h_ref[2 * i + k] = hz
            f = hz.astype(F32)
            for half in range(2):
                r = f[half * 64 : half * 64 + 64]
                parts.append((r[0:16] + r[16:32]) + (r[32:48] + r[48:64]))
        hi = [p.astype(BF) for p in parts]
        lo = [(p - q.astype(F32)).astype(BF) for p, q in zip(parts, hi)]
        acc_ref[pl.ds(pl.multiple_of(i * 16, 16), 16), :] = jnp.concatenate(hi + lo, axis=1)

    run_conv(lambda z: stage(z, at_ref, x_ref, top_ref, bot_ref, tl_ref, tr_ref, s_ref), finish, w_ref, s_ref)
    r, lane = iota((1024, 128), 0) % 512, iota((1024, 128), 1)
    pick = jnp.where((r // 128) * 32 + (r % 128) // 4 == lane, 0.0625, 0.0).astype(BF)
    pooled = mm(acc_ref[...], pick).astype(BF)
    nothing = jnp.zeros((16, 128), BF)
    a, b = at_ref[0], at_ref[1]
    for to in range(4):
        goes = (a == to) | ((a == to - 1) & (b == 7)) | ((a == to + 1) & (b == 0))
        sent = kept(goes, pooled)
        for slab in range(32):
            for j in range(3):
                at = slab + j - 1
                block = sent[at * 16 : at * 16 + 16] if 0 <= at < 32 else nothing
                p_ref[slab, to, j * 16 : j * 16 + 16, :] = block
    total = jnp.zeros((128, 128), F32)
    for g in range(8):
        total = total + outer_columns(jnp.concatenate([h_ref[g * 8 + k] for k in range(8)], axis=1), g * 8)
    cols_ref[...] = total.astype(BF)


def fine_scratch():
    return [
        pltpu.VMEM((66 * 512, 128), BF),
        pltpu.VMEM((128, 1536), BF),
        pltpu.VMEM((16, 1536), F32),
        pltpu.VMEM((160, 128), BF),
        pltpu.VMEM((160, 128), BF),
    ]


def fine1(at, x, top, bot, cl, cr, k, b):
    return pl.pallas_call(
        fine1_body,
        in_specs=[pl.BlockSpec(memory_space=pltpu.SMEM)] + vm(7),
        out_specs=vm(3),
        out_shape=[
            jax.ShapeDtypeStruct((64, 128, 128), BF),
            jax.ShapeDtypeStruct((32, 4, 48, 128), BF),
            jax.ShapeDtypeStruct((128, 128), BF),
        ],
        scratch_shapes=fine_scratch() + [pltpu.VMEM((512, 1024), BF)],
        interpret=INTERPRET,
        name="fine1",
    )(at, x, top, bot, cl, cr, k, b)


def fine2_body(at_ref, x_ref, top_ref, bot_ref, cl_ref, cr_ref, k_ref, b_ref, c_ref, o_ref, s_ref, w_ref, w0_ref, tl_ref, tr_ref):
    fine_setup(at_ref, k_ref, top_ref, bot_ref, cl_ref, cr_ref, w_ref, w0_ref, s_ref, tl_ref, tr_ref, True)
    bias = bias_rows(b_ref, True)
    r, lane = iota((128, 512), 0), iota((128, 512), 1)
    up = onehot((lane // 128) * 32 + (lane % 128) // 4 == r)
    for g in range(4):
        e = mm(c_ref[g * 8 : g * 8 + 8].reshape(128, 128), up).astype(BF)
        for p in range(8):
            for q in range(4):
                z = 2 * (g * 8 + p) + q // 2
                row = (z + 1) * 512 + 480 + (q % 2) * 16
                s_ref[row : row + 16, :] = e[p * 16 : p * 16 + 16, q * 128 : q * 128 + 128]
    rr, kk = iota((128, 32), 0), iota((128, 32), 1)
    w_ref[:, 992:1024] = onehot((kk % 16 == rr // 8) & (kk // 16 == (rr % 8) // 4))

    def finish(i, out):
        v = out + bias
        for k in range(2):
            o_ref[:, 2 * i + k] = v[:, k * 128 : (k + 1) * 128].reshape(16, 8, 128).astype(BF)

    run_conv(lambda z: stage(z, at_ref, x_ref, top_ref, bot_ref, tl_ref, tr_ref, s_ref), finish, w_ref, s_ref)


def fine2(at, x, top, bot, cl, cr, k, b, c):
    def whole(*shape):
        return pl.BlockSpec(shape, lambda i, at: (0,) * len(shape))

    return pl.pallas_call(
        fine2_body,
        grid_spec=pltpu.PrefetchScalarGridSpec(
            num_scalar_prefetch=1,
            grid=(1,),
            in_specs=[
                whole(64, 128, 128),
                whole(1056, 128),
                whole(1056, 128),
                whole(128, 128),
                whole(128, 128),
                whole(27, 16, 16),
                whole(1, 16),
                pl.BlockSpec((32, 1, 16, 128), lambda i, at: (0, at[0], 0, 0)),
            ],
            out_specs=whole(16, 64, 8, 128),
            scratch_shapes=fine_scratch(),
        ),
        out_shape=jax.ShapeDtypeStruct((16, 64, 8, 128), BF),
        interpret=INTERPRET,
        name="fine2",
    )(at, x, top, bot, cl, cr, k, b, c)


def spread_x(v):
    lane = iota(v.shape, 1)
    left = jnp.where(lane == 0, jnp.zeros((), BF), pltpu.roll(v, 1, 1))
    right = jnp.where(lane == 127, jnp.zeros((), BF), pltpu.roll(v, 127, 1))
    return jnp.concatenate([left, v, right], axis=0)


def window(s_ref, z, y, rows, per_z):
    both = []
    for k in range(2):
        parts = [
            s_ref[pl.ds(pl.multiple_of((z + dz) * per_z + (y + k) * rows, 16), 3 * rows), :] for dz in range(3)
        ]
        both.append(jnp.concatenate(parts, axis=0))
    return jnp.concatenate(both, axis=1)


def conv1a_body(masked, at_ref, first_ref, second_ref, k_ref, b_ref, o_ref, s_ref, w_ref):
    swap = at_ref[4] == 1
    reaches = at_ref[5] == 1
    for t in range(27):
        w_ref[:, t * 64 : t * 64 + 64] = k_ref[t][:, 0:64]

    def fill(y, _):
        for zi in range(2):
            a, b = first_ref[zi, y], second_ref[zi, y]
            if masked:
                a = kept(reaches, a)
            for at, v in ((zi, jnp.where(swap, b, a)), (zi + 2, jnp.where(swap, a, b))):
                s_ref[pl.ds(pl.multiple_of(at * 3840 + y * 192, 64), 192), :] = spread_x(v)
        return 0

    lax.fori_loop(0, 20, fill, 0)
    bias = b_ref[...]

    def step(i, _):
        outs = [
            mm(w_ref[...], window(s_ref, zo, 6 * i + 2 * k, 192, 3840)) + bias for zo in range(2) for k in range(3)
        ]
        for j in range(6):
            o_ref[j // 3 * 9 + 3 * i + j % 3] = outs[j]
        return 0

    lax.fori_loop(0, 3, step, 0)


def conv1a(at, first, second, k, b, name):
    return pl.pallas_call(
        functools.partial(conv1a_body, name == "distant"),
        in_specs=[pl.BlockSpec(memory_space=pltpu.SMEM)] + vm(4),
        out_specs=vm(1)[0],
        out_shape=jax.ShapeDtypeStruct((18, 64, 256), F32),
        scratch_shapes=[pltpu.VMEM((4 * 20 * 192, 128), BF), pltpu.VMEM((64, 1728), BF)],
        interpret=INTERPRET,
    )(at, first, second, k, b)


def coarse_body(at_ref, main_ref, lo_ref, hi_ref, near_ref, far_ref, k1_ref, k2_ref, b_ref, proj_ref, out_ref, ctx_ref, sp_ref, sm_ref, w1_ref, w2_ref, co_ref, ct_ref):
    n, w = at_ref[2], at_ref[3]
    odd = at_ref[4] == 1
    for t in range(27):
        w1_ref[:, t * 16 : t * 16 + 16] = k1_ref[t][:, 64:80]
        w2_ref[:, t * 64 : t * 64 + 64] = k2_ref[t]
    r, c = iota((512, 512), 0), iota((512, 512), 1)
    order = onehot((r % 128 // 32 == c // 128) & (r // 128 == c % 128 // 32) & (r % 32 == c % 32))
    for wb in range(10):
        if wb == 0:
            blocks = [jnp.where(n > 0, lo_ref[0, k], jnp.zeros((48, 128), BF)) for k in range(4)]
        elif wb == 9:
            blocks = [jnp.where(n < 3, hi_ref[0, k], jnp.zeros((48, 128), BF)) for k in range(4)]
        else:
            blocks = [main_ref[wb - 1, k] for k in range(4)]
        t = mm(jnp.concatenate(blocks, axis=1), order).astype(BF)
        for s in range(3):
            for zi in range(4):
                v = t[s * 16 : s * 16 + 16, zi * 128 : zi * 128 + 128]
                base = (2 * s + zi // 2) * 960 + (2 * wb + zi % 2) * 48
                sp_ref[base : base + 48, :] = spread_x(v)

    def mid(yp, _):
        outs = []
        for zo in range(4):
            i = zo % 2 * 9 + yp
            low, high = (far_ref, near_ref) if zo < 2 else (near_ref, far_ref)
            part = jnp.where(odd, high[i], low[i])
            outs.append(mm(w1_ref[...], window(sp_ref, zo, 2 * yp, 48, 960)) + part)
        keep = [(yp > 0) | (n > 0), (yp < 8) | (n < 3)]
        for zo in range(4):
            v = jnp.maximum(outs[zo], 0.0)
            for k in range(2):
                inside = keep[k] & (w > 0) if zo == 0 else keep[k] & (w < 31) if zo == 3 else keep[k]
                m = jnp.where(inside, v[:, k * 128 : k * 128 + 128], 0.0).astype(BF)
                sm_ref[pl.ds(pl.multiple_of(zo * 3456 + (2 * yp + k) * 192, 64), 192), :] = spread_x(m)
        return 0

    lax.fori_loop(0, 9, mid, 0)
    bias = b_ref[...]
    proj = proj_ref[...]

    def last(i, _):
        outs = [mm(w2_ref[...], window(sm_ref, z, 4 * i + 2 * h, 192, 3456)) for z in range(2) for h in range(2)]
        for j in range(4):
            z, b = j // 2, 2 * i + j % 2
            o = jnp.maximum(outs[j] + bias, 0.0).astype(BF)
            ct = mm(proj, o).astype(BF)
            for k in range(2):
                lanes = slice(k * 128, k * 128 + 128)
                co_ref[pl.ds(pl.multiple_of((2 * b + k) * 64, 64), 64), z * 128 : z * 128 + 128] = o[:, lanes]
                at = (z * 2 + k) * 128
                ct_ref[pl.ds(pl.multiple_of(b * 16, 16), 16), at : at + 128] = ct[:, lanes]
        return 0

    lax.fori_loop(0, 4, last, 0)
    back = onehot((c % 128 // 32 == r // 128) & (c // 128 == r % 128 // 32) & (r % 32 == c % 32))
    ct = mm(ct_ref[...], back).astype(BF)
    for b in range(8):
        for k in range(4):
            block = ct[b * 16 : b * 16 + 16, k * 128 : k * 128 + 128]
            for to in range(4):
                ctx_ref[to, b, k] = jnp.where(n == to, block, jnp.zeros((), BF))
    r, k = iota((256, 256), 0), iota((256, 256), 1)
    perm = onehot((r % 16) * 16 + r // 16 == k)
    for g in range(4):
        rows = jnp.concatenate([co_ref[y * 64 + g * 16 : y * 64 + g * 16 + 16, :] for y in range(16)], axis=0)
        o = mm(perm, rows).astype(BF)
        for z in range(2):
            out_ref[g * 16 : g * 16 + 16, z] = o[:, z * 128 : z * 128 + 128].reshape(16, 16, 128)


def coarse(at, got, near, far, k1, k2, b2, proj):
    def whole(shape):
        return pl.BlockSpec(shape, lambda i, at: (0,) * len(shape))

    return pl.pallas_call(
        coarse_body,
        grid_spec=pltpu.PrefetchScalarGridSpec(
            num_scalar_prefetch=1,
            grid=(1,),
            in_specs=[
                pl.BlockSpec((8, 4, 48, 128), lambda i, at: (at[2], 0, 0, 0)),
                pl.BlockSpec((1, 4, 48, 128), lambda i, at: (jnp.maximum(8 * at[2] - 1, 0), 0, 0, 0)),
                pl.BlockSpec((1, 4, 48, 128), lambda i, at: (jnp.minimum(8 * at[2] + 8, 31), 0, 0, 0)),
                whole((18, 64, 256)),
                whole((18, 64, 256)),
                whole((27, 64, 80)),
                whole((27, 64, 64)),
                whole((64, 1)),
                whole((16, 64)),
            ],
            out_specs=[whole((64, 2, 16, 128)), whole((4, 8, 4, 16, 128))],
            scratch_shapes=[
                pltpu.VMEM((6 * 20 * 48, 128), BF),
                pltpu.VMEM((4 * 18 * 192, 128), BF),
                pltpu.VMEM((64, 432), BF),
                pltpu.VMEM((64, 1728), BF),
                pltpu.VMEM((1024, 256), BF),
                pltpu.VMEM((128, 512), BF),
            ],
        ),
        out_shape=[
            jax.ShapeDtypeStruct((64, 2, 16, 128), BF),
            jax.ShapeDtypeStruct((4, 8, 4, 16, 128), BF),
        ],
        interpret=INTERPRET,
        name="coarse",
    )(at, got, got, got, near, far, k1, k2, b2, proj)


def shift(array, axis, by):
    count = lax.axis_size(axis)
    return lax.ppermute(array, axis, [(i, (i + by) % count) for i in range(count)])


def across_y(rows, from_left, from_right):
    down = jnp.concatenate([rows[:, 112:128, :].reshape(1024, 128), from_left[112:128], from_right[112:128]], axis=0)
    up = jnp.concatenate([rows[:, 0:16, :].reshape(1024, 128), from_left[0:16], from_right[0:16]], axis=0)
    return shift(down, "wide", 1), shift(up, "wide", -1)


def taps(w):
    return jnp.transpose(w, (2, 3, 4, 0, 1)).reshape(27, w.shape[0], w.shape[1])


def local(
    fine_in,
    coarse_in,
    w_fine1,
    b_fine1,
    w_fine2,
    b_fine2,
    w_coarse1,
    b_coarse1,
    w_coarse2,
    b_coarse2,
    w_proj,
):
    w = lax.axis_index("wide")
    n = lax.axis_index("narrow")
    reaches = jnp.where(w % 2 == 1, w < 31, w > 0).astype(jnp.int32)
    at = jnp.stack([w // 8, w % 8, n, w, w % 2, reaches])
    rows, cols = prep(fine_in)
    ct = cprep(coarse_in)
    east = jnp.concatenate([cols, ct[:, 14:16].reshape(256, 128)], axis=0)
    west = jnp.concatenate([cols, ct[:, 0:2].reshape(256, 128)], axis=0)
    from_left = shift(east, "narrow", 1)
    from_right = shift(west, "narrow", -1)
    top, bottom = across_y(rows, from_left, from_right)
    slab = jnp.concatenate(
        [
            jnp.where(n > 0, from_left[128:], jnp.zeros((), BF)).reshape(2, 2, 64, 128),
            ct,
            jnp.where(n < 3, from_right[128:], jnp.zeros((), BF)).reshape(2, 2, 64, 128),
        ],
        axis=1,
    )
    mate = lax.ppermute(slab, "wide", [(i, i ^ 1) for i in range(32)])
    hops = [(i, i + 2 - 4 * (i % 2)) for i in range(32)]
    far = lax.ppermute(mate, "wide", [(i, j % 32) for i, j in hops])
    hidden, parcels, hcols = fine1(
        at, rows, top, bottom, from_left, from_right, taps(w_fine1), b_fine1[None]
    )
    got = lax.all_to_all(parcels.reshape(128, 48, 128), ("wide", "narrow"), 0, 0, tiled=True)
    near_part = conv1a(at, slab, mate, taps(w_coarse1), b_coarse1[:, None], "near")
    hleft = shift(hcols, "narrow", 1)
    hright = shift(hcols, "narrow", -1)
    htop, hbottom = across_y(hidden, hleft, hright)
    far_part = conv1a(at, far, slab, taps(w_coarse1), b_coarse1[:, None], "distant")
    coarse_out, context = coarse(
        at,
        got.reshape(32, 4, 48, 128),
        near_part,
        far_part,
        taps(w_coarse1),
        taps(w_coarse2),
        b_coarse2[:, None],
        w_proj,
    )
    arrived = lax.all_to_all(context.reshape(128, 16, 128), ("wide", "narrow"), 0, 0, tiled=True)
    fine_out = fine2(
        at,
        hidden,
        htop,
        hbottom,
        hleft,
        hright,
        taps(w_fine2),
        b_fine2[None],
        arrived.reshape(32, 4, 16, 128),
    )
    return fine_out, coarse_out


def solution(mesh):
    return jax.shard_map(
        local,
        mesh=mesh,
        in_specs=(P(None, None, "wide", "narrow"), P(None, "wide", "narrow", None)) + (P(),) * 9,
        out_specs=(P(None, None, "wide", "narrow"), P(None, "wide", "narrow", None)),
        check_vma=False,
    )
```

```python
import functools

import jax
import jax.numpy as jnp
from jax import lax
from jax.experimental import pallas as pl
from jax.experimental.pallas import tpu as pltpu
from jax.sharding import PartitionSpec as P


BF = jnp.bfloat16
F32 = jnp.float32
TERM = jnp.bfloat16
INTERPRET = False


def iota(shape, axis):
    return lax.broadcasted_iota(jnp.int32, shape, axis)


def onehot(mask):
    return jnp.where(mask, 1.0, 0.0).astype(BF)


def mm(a, b):
    return jnp.dot(a, b, preferred_element_type=F32)


def vm(n):
    return [pl.BlockSpec(memory_space=pltpu.VMEM)] * n


def outer_columns(rows, first_z):
    shape = (rows.shape[1], 128)
    r, lane = iota(shape, 0), iota(shape, 1)
    z, x = first_z + r // 128, r % 128
    return mm(rows, onehot(((x == 0) & (lane == z)) | ((x == 127) & (lane == z + 64))))


def prep_body(x_ref, t_ref, down_ref, up_ref, cols_ref, acc_ref):
    step = pl.program_id(0)
    zb = t_ref.shape[0]
    r, k = iota((128, 128), 0), iota((128, 128), 1)
    perm = onehot((r % 16) * 8 + r // 16 == k)
    rows = []
    for i in range(0, zb, 2):
        pair = jnp.concatenate([x_ref[:, step * zb + i + j].reshape(128, 128) for j in range(2)], axis=1)
        out = mm(perm, pair).astype(BF)
        for j in range(2):
            v = out[:, j * 128 : j * 128 + 128]
            t_ref[i + j] = v
            down_ref[(i + j) * 16 : (i + j) * 16 + 16, :] = v[112:128]
            up_ref[(i + j) * 16 : (i + j) * 16 + 16, :] = v[0:16]
        rows.append(out)
    part = outer_columns(jnp.concatenate(rows, axis=1), step * zb)

    @pl.when(step == 0)
    def _():
        acc_ref[...] = part

    @pl.when(step > 0)
    def _():
        acc_ref[...] += part

    cols_ref[...] = acc_ref[...].astype(BF)


def prep(x):
    zb = 8
    return pl.pallas_call(
        prep_body,
        grid=(64 // zb,),
        in_specs=[pl.BlockSpec((16, 64, 8, 128), lambda i: (0, 0, 0, 0))],
        out_specs=[
            pl.BlockSpec((zb, 128, 128), lambda i: (i, 0, 0)),
            pl.BlockSpec((zb * 16, 128), lambda i: (i, 0)),
            pl.BlockSpec((zb * 16, 128), lambda i: (i, 0)),
            pl.BlockSpec((128, 128), lambda i: (0, 0)),
        ],
        out_shape=[
            jax.ShapeDtypeStruct((64, 128, 128), BF),
            jax.ShapeDtypeStruct((1056, 128), BF),
            jax.ShapeDtypeStruct((1056, 128), BF),
            jax.ShapeDtypeStruct((128, 128), BF),
        ],
        scratch_shapes=[pltpu.VMEM((128, 128), F32)],
        interpret=INTERPRET,
        name="prep",
    )(x)


def cprep_body(x_ref, cols_ref, o_ref, east_ref, west_ref):
    east_ref[0:128, :] = cols_ref[...]
    west_ref[0:128, :] = cols_ref[...]
    r, k = iota((256, 256), 0), iota((256, 256), 1)
    perm = onehot((r % 16) * 16 + r // 16 == k)
    for g in range(4):
        pair = jnp.concatenate(
            [x_ref[g * 16 : g * 16 + 16, z].reshape(256, 128) for z in range(2)], axis=1
        )
        out = mm(perm, pair).astype(BF)
        for z in range(2):
            for y in range(16):
                v = out[y * 16 : y * 16 + 16, z * 128 : z * 128 + 128]
                o_ref[z, y, g * 16 : g * 16 + 16, :] = v
                row = 128 + z * 128 + (y % 2) * 64 + g * 16
                if y >= 14:
                    east_ref[row : row + 16, :] = v
                if y < 2:
                    west_ref[row : row + 16, :] = v


def cprep(x, cols):
    return pl.pallas_call(
        cprep_body,
        in_specs=vm(2),
        out_specs=vm(3),
        out_shape=[
            jax.ShapeDtypeStruct((2, 16, 64, 128), BF),
            jax.ShapeDtypeStruct((384, 128), BF),
            jax.ShapeDtypeStruct((384, 128), BF),
        ],
        interpret=INTERPRET,
        name="cprep",
    )(x, cols)


def weights_body(f1_ref, f2_ref, c1_ref, c2_ref, wf1_ref, wf2_ref, wa_ref, wb_ref, wc_ref, w0_ref):
    for k_ref, w_ref in ((f1_ref, wf1_ref), (f2_ref, wf2_ref)):
        w0_ref[...] = jnp.zeros((16, 1536), F32)
        for t in range(27):
            dz, dy, dx = t // 9, t // 3 % 3, t % 3
            at = dz * 512 + dx * 160 + dy * 16
            w0_ref[:, at : at + 16] = k_ref[t].astype(F32)
        w0 = w0_ref[...]
        for y in range(8):
            w_ref[y * 16 : y * 16 + 16, :] = (pltpu.roll(w0, y * 16, 1) if y else w0).astype(BF)
    r, k = iota((128, 128), 0), iota((128, 128), 1)
    wf2_ref[...] = mm(onehot((r % 8) * 16 + r // 8 == k), wf2_ref[...]).astype(BF)
    for t in range(27):
        both = c1_ref[t]
        wa_ref[:, t * 64 : t * 64 + 64] = both[:, 0:64]
        wb_ref[:, t * 16 : t * 16 + 16] = both[:, 64:80]
        wc_ref[:, t * 64 : t * 64 + 64] = c2_ref[t]


def weights(f1, f2, c1, c2):
    return pl.pallas_call(
        weights_body,
        in_specs=vm(4),
        out_specs=vm(5),
        out_shape=[
            jax.ShapeDtypeStruct((128, 1536), BF),
            jax.ShapeDtypeStruct((128, 1536), BF),
            jax.ShapeDtypeStruct((64, 1728), BF),
            jax.ShapeDtypeStruct((64, 432), BF),
            jax.ShapeDtypeStruct((64, 1728), BF),
        ],
        scratch_shapes=[pltpu.VMEM((16, 1536), F32)],
        interpret=INTERPRET,
        name="weights",
    )(f1, f2, c1, c2)


def kept(ok, v):
    return jnp.where(ok, v, jnp.zeros((), BF))


def stage(z, at_ref, x_ref, top_ref, bot_ref, tl_ref, tr_ref, s_ref):
    rows = pl.ds(pl.multiple_of(z * 16, 16), 16)
    top = kept(at_ref[3] > 0, top_ref[rows, :])
    bot = kept(at_ref[3] < 31, bot_ref[rows, :])
    v = jnp.concatenate([top, x_ref[z], bot], axis=0)
    lane = iota((160, 128), 1)
    left = jnp.where(lane == 0, pltpu.roll(tl_ref[...], lax.rem(192 - z, 128), 1), pltpu.roll(v, 1, 1))
    right = jnp.where(lane == 127, pltpu.roll(tr_ref[...], 127 - z, 1), pltpu.roll(v, 127, 1))
    base = pl.multiple_of((z + 1) * 512, 512)
    s_ref[pl.ds(base, 160), :] = left
    s_ref[pl.ds(base + 160, 160), :] = v
    s_ref[pl.ds(base + 320, 160), :] = right


def conv_pair(z, w_ref, s_ref):
    base = pl.multiple_of(z * 512, 512)
    rhs = jnp.concatenate([s_ref[pl.ds(base, 1536), :], s_ref[pl.ds(base + 512, 1536), :]], axis=1)
    return mm(w_ref[...], rhs)


def bias_rows(b_ref, count, row_of):
    shape = (count, b_ref.shape[1])
    r, k = iota(shape, 0), iota(shape, 1)
    return jnp.sum(jnp.where(row_of(r) == k, b_ref[...], 0.0), axis=1, keepdims=True)


def fine_setup(at_ref, top_ref, bot_ref, cl_ref, cr_ref, s_ref, tl_ref, tr_ref):
    n, w = at_ref[2], at_ref[3]
    for ref, edge, col, ok in ((tl_ref, 1024, cl_ref, n > 0), (tr_ref, 1040, cr_ref, n < 3)):
        ref[0:16, :] = kept(ok & (w > 0), top_ref[edge : edge + 16, :])
        ref[16:144, :] = kept(ok, col[0:128, :])
        ref[144:160, :] = kept(ok & (w < 31), bot_ref[edge : edge + 16, :])
    s_ref[0:512, :] = jnp.zeros((512, 128), BF)
    s_ref[65 * 512 : 66 * 512, :] = jnp.zeros((512, 128), BF)
    for z in range(1, 65):
        s_ref[z * 512 + 480 : z * 512 + 512, :] = jnp.zeros((32, 128), BF)


def run_conv(stage_fn, finish, w_ref, s_ref):
    for z in range(5):
        stage_fn(z)

    def step(i, _):
        first = conv_pair(4 * i, w_ref, s_ref)
        second = conv_pair(4 * i + 2, w_ref, s_ref)
        for k in range(5, 9):
            stage_fn(4 * i + k)
        finish(2 * i, first)
        finish(2 * i + 1, second)
        return 0

    lax.fori_loop(0, 14, step, 0)
    first = conv_pair(56, w_ref, s_ref)
    second = conv_pair(58, w_ref, s_ref)
    for k in range(61, 64):
        stage_fn(k)
    finish(28, first)
    finish(29, second)
    first = conv_pair(60, w_ref, s_ref)
    second = conv_pair(62, w_ref, s_ref)
    finish(30, first)
    finish(31, second)


def fine1_body(at_ref, x_ref, top_ref, bot_ref, cl_ref, cr_ref, w_ref, b_ref, h_ref, p_ref, cols_ref, down_ref, up_ref, s_ref, tl_ref, tr_ref, acc_ref):
    fine_setup(at_ref, top_ref, bot_ref, cl_ref, cr_ref, s_ref, tl_ref, tr_ref)
    bias = bias_rows(b_ref, 128, lambda r: r % 16)

    def finish(i, out):
        h = jnp.maximum(out + bias, 0.0).astype(BF)
        parts = []
        for k in range(2):
            hz = h[:, k * 128 : (k + 1) * 128]
            h_ref[2 * i + k] = hz
            row = pl.ds(pl.multiple_of((2 * i + k) * 16, 16), 16)
            down_ref[row, :] = hz[112:128]
            up_ref[row, :] = hz[0:16]
            f = hz.astype(F32)
            for half in range(2):
                r = f[half * 64 : half * 64 + 64]
                parts.append((r[0:16] + r[16:32]) + (r[32:48] + r[48:64]))
        hi = [p.astype(BF) for p in parts]
        lo = [(p - q.astype(F32)).astype(BF) for p, q in zip(parts, hi)]
        acc_ref[pl.ds(pl.multiple_of(i * 16, 16), 16), :] = jnp.concatenate(hi + lo, axis=1)

    run_conv(lambda z: stage(z, at_ref, x_ref, top_ref, bot_ref, tl_ref, tr_ref, s_ref), finish, w_ref, s_ref)
    r, lane = iota((1024, 128), 0) % 512, iota((1024, 128), 1)
    pick = jnp.where((r // 128) * 32 + (r % 128) // 4 == lane, 0.0625, 0.0).astype(BF)
    p_ref[...] = mm(acc_ref[...], pick).astype(BF)
    total = jnp.zeros((128, 128), F32)
    for g in range(8):
        total = total + outer_columns(jnp.concatenate([h_ref[g * 8 + k] for k in range(8)], axis=1), g * 8)
    cols_ref[...] = total.astype(BF)


def fine_scratch():
    return [
        pltpu.VMEM((66 * 512, 128), BF),
        pltpu.VMEM((160, 128), BF),
        pltpu.VMEM((160, 128), BF),
    ]


def fine1(at, x, top, bot, cl, cr, w, b):
    return pl.pallas_call(
        fine1_body,
        in_specs=[pl.BlockSpec(memory_space=pltpu.SMEM)] + vm(7),
        out_specs=vm(5),
        out_shape=[
            jax.ShapeDtypeStruct((64, 128, 128), BF),
            jax.ShapeDtypeStruct((512, 128), BF),
            jax.ShapeDtypeStruct((128, 128), BF),
            jax.ShapeDtypeStruct((1056, 128), BF),
            jax.ShapeDtypeStruct((1056, 128), BF),
        ],
        scratch_shapes=fine_scratch() + [pltpu.VMEM((512, 1024), BF)],
        interpret=INTERPRET,
        name="fine1",
    )(at, x, top, bot, cl, cr, w, b)


def fine2_body(at_ref, x_ref, top_ref, bot_ref, cl_ref, cr_ref, w_ref, b_ref, o_ref, s_ref, tl_ref, tr_ref):
    fine_setup(at_ref, top_ref, bot_ref, cl_ref, cr_ref, s_ref, tl_ref, tr_ref)
    bias = bias_rows(b_ref, 128, lambda r: r // 8)

    def finish(i, out):
        v = (out + bias).astype(TERM)
        for k in range(2):
            o_ref[2 * i + k] = v[:, k * 128 : (k + 1) * 128]

    run_conv(lambda z: stage(z, at_ref, x_ref, top_ref, bot_ref, tl_ref, tr_ref, s_ref), finish, w_ref, s_ref)


def fine2(at, x, top, bot, cl, cr, w, b):
    return pl.pallas_call(
        fine2_body,
        in_specs=[pl.BlockSpec(memory_space=pltpu.SMEM)] + vm(7),
        out_specs=vm(1)[0],
        out_shape=jax.ShapeDtypeStruct((64, 128, 128), TERM),
        scratch_shapes=fine_scratch(),
        interpret=INTERPRET,
        name="fine2",
    )(at, x, top, bot, cl, cr, w, b)


def final_body(at_ref, t_ref, c_ref, o_ref):
    r, lane = iota((128, 512), 0), iota((128, 512), 1)
    up = onehot((lane // 128) * 32 + (lane % 128) // 4 == r)
    e = mm(c_ref[...].reshape(128, 128), up).astype(BF)
    rr, kk = iota((128, 32), 0), iota((128, 32), 1)
    widen = onehot((kk % 16 == rr // 8) & (kk // 16 == (rr % 8) // 4))
    both = []
    for p in range(8):
        row = e[p * 16 : p * 16 + 16]
        for k in range(2):
            both.append(
                jnp.concatenate([row[:, k * 256 : k * 256 + 128], row[:, k * 256 + 128 : k * 256 + 256]], axis=0)
            )
    c = mm(widen, jnp.concatenate(both, axis=1))
    for z in range(16):
        v = t_ref[z].astype(F32) + c[:, z * 128 : z * 128 + 128]
        o_ref[:, z] = v.reshape(16, 8, 128).astype(BF)


def final(at, t, c):
    return pl.pallas_call(
        final_body,
        grid_spec=pltpu.PrefetchScalarGridSpec(
            num_scalar_prefetch=1,
            grid=(4,),
            in_specs=[
                pl.BlockSpec((16, 128, 128), lambda i, at: (i, 0, 0)),
                pl.BlockSpec((8, 1, 16, 128), lambda i, at: (i, at[0], 0, 0)),
            ],
            out_specs=pl.BlockSpec((16, 16, 8, 128), lambda i, at: (0, i, 0, 0)),
        ),
        out_shape=jax.ShapeDtypeStruct((16, 64, 8, 128), BF),
        interpret=INTERPRET,
        name="final",
    )(at, t, c)


def spread_x(v):
    lane = iota(v.shape, 1)
    left = jnp.where(lane == 0, jnp.zeros((), BF), pltpu.roll(v, 1, 1))
    right = jnp.where(lane == 127, jnp.zeros((), BF), pltpu.roll(v, 127, 1))
    return jnp.concatenate([left, v, right], axis=0)


def window(s_ref, z, y, rows, per_z):
    both = []
    for k in range(2):
        parts = [
            s_ref[pl.ds(pl.multiple_of((z + dz) * per_z + (y + k) * rows, 16), 3 * rows), :] for dz in range(3)
        ]
        both.append(jnp.concatenate(parts, axis=0))
    return jnp.concatenate(both, axis=1)


def conv1a_body(masked, at_ref, first_ref, second_ref, w_ref, b_ref, o_ref, s_ref):
    swap = at_ref[4] == 1
    reaches = at_ref[5] == 1

    def fill(y, _):
        for zi in range(2):
            a, b = first_ref[zi, y], second_ref[zi, y]
            if masked:
                a = kept(reaches, a)
            for at, v in ((zi, jnp.where(swap, b, a)), (zi + 2, jnp.where(swap, a, b))):
                s_ref[pl.ds(pl.multiple_of(at * 3840 + y * 192, 64), 192), :] = spread_x(v)
        return 0

    lax.fori_loop(0, 20, fill, 0)
    bias = bias_rows(b_ref, 64, lambda r: r)

    def step(i, _):
        outs = [
            mm(w_ref[...], window(s_ref, zo, 6 * i + 2 * k, 192, 3840)) + bias for zo in range(2) for k in range(3)
        ]
        for j in range(6):
            o_ref[j // 3 * 9 + 3 * i + j % 3] = outs[j]
        return 0

    lax.fori_loop(0, 3, step, 0)


def conv1a(at, first, second, w, b, name):
    return pl.pallas_call(
        functools.partial(conv1a_body, name == "distant"),
        in_specs=[pl.BlockSpec(memory_space=pltpu.SMEM)] + vm(4),
        out_specs=vm(1)[0],
        out_shape=jax.ShapeDtypeStruct((18, 64, 256), F32),
        scratch_shapes=[pltpu.VMEM((4 * 20 * 192, 128), BF)],
        interpret=INTERPRET,
    )(at, first, second, w, b)


def coarse_body(at_ref, got_ref, near_ref, far_ref, w1_ref, w2_ref, b_ref, proj_ref, out_ref, ctx_ref, sp_ref, sm_ref, co_ref, ct_ref):
    n, w = at_ref[2], at_ref[3]
    odd = at_ref[4] == 1
    r, c = iota((512, 512), 0), iota((512, 512), 1)
    order = onehot((r % 128 // 32 == c // 128) & (r // 128 == c % 128 // 32) & (r % 32 == c % 32))
    for wb in range(10):
        if wb == 0:
            blocks = [kept(n > 0, got_ref[8 * k + 7, 1]) for k in range(4)]
        elif wb == 9:
            blocks = [kept(n < 3, got_ref[8 * k, 1]) for k in range(4)]
        else:
            blocks = [got_ref[8 * k + wb - 1, 0] for k in range(4)]
        t = mm(jnp.concatenate(blocks, axis=1), order).astype(BF)
        for s in range(3):
            for zi in range(4):
                v = t[s * 16 : s * 16 + 16, zi * 128 : zi * 128 + 128]
                base = (2 * s + zi // 2) * 960 + (2 * wb + zi % 2) * 48
                sp_ref[base : base + 48, :] = spread_x(v)

    def mid(yp, _):
        outs = []
        for zo in range(4):
            i = zo % 2 * 9 + yp
            low, high = (far_ref, near_ref) if zo < 2 else (near_ref, far_ref)
            part = jnp.where(odd, high[i], low[i])
            outs.append(mm(w1_ref[...], window(sp_ref, zo, 2 * yp, 48, 960)) + part)
        keep = [(yp > 0) | (n > 0), (yp < 8) | (n < 3)]
        for zo in range(4):
            v = jnp.maximum(outs[zo], 0.0)
            for k in range(2):
                inside = keep[k] & (w > 0) if zo == 0 else keep[k] & (w < 31) if zo == 3 else keep[k]
                m = jnp.where(inside, v[:, k * 128 : k * 128 + 128], 0.0).astype(BF)
                sm_ref[pl.ds(pl.multiple_of(zo * 3456 + (2 * yp + k) * 192, 64), 192), :] = spread_x(m)
        return 0

    lax.fori_loop(0, 9, mid, 0)
    bias = bias_rows(b_ref, 64, lambda r: r)
    proj = proj_ref[...]

    def last(i, _):
        outs = [mm(w2_ref[...], window(sm_ref, z, 4 * i + 2 * h, 192, 3456)) for z in range(2) for h in range(2)]
        for j in range(4):
            z, b = j // 2, 2 * i + j % 2
            o = jnp.maximum(outs[j] + bias, 0.0).astype(BF)
            ct = mm(proj, o).astype(BF)
            for k in range(2):
                lanes = slice(k * 128, k * 128 + 128)
                co_ref[pl.ds(pl.multiple_of((2 * b + k) * 64, 64), 64), z * 128 : z * 128 + 128] = o[:, lanes]
                at = (z * 2 + k) * 128
                ct_ref[pl.ds(pl.multiple_of(b * 16, 16), 16), at : at + 128] = ct[:, lanes]
        return 0

    lax.fori_loop(0, 4, last, 0)
    back = onehot((c % 128 // 32 == r // 128) & (c // 128 == r % 128 // 32) & (r % 32 == c % 32))
    ct = mm(ct_ref[...], back).astype(BF)
    for b in range(8):
        for k in range(4):
            block = ct[b * 16 : b * 16 + 16, k * 128 : k * 128 + 128]
            for to in range(4):
                ctx_ref[to, b, k] = jnp.where(n == to, block, jnp.zeros((), BF))
    r, k = iota((256, 256), 0), iota((256, 256), 1)
    perm = onehot((r % 16) * 16 + r // 16 == k)
    for g in range(4):
        rows = jnp.concatenate([co_ref[y * 64 + g * 16 : y * 64 + g * 16 + 16, :] for y in range(16)], axis=0)
        o = mm(perm, rows).astype(BF)
        for z in range(2):
            out_ref[g * 16 : g * 16 + 16, z] = o[:, z * 128 : z * 128 + 128].reshape(16, 16, 128)


def coarse(at, got, near, far, w1, w2, b2, proj):
    def whole(shape):
        return pl.BlockSpec(shape, lambda i, at: (0,) * len(shape))

    return pl.pallas_call(
        coarse_body,
        grid_spec=pltpu.PrefetchScalarGridSpec(
            num_scalar_prefetch=1,
            grid=(1,),
            in_specs=[
                whole((32, 2, 48, 128)),
                whole((18, 64, 256)),
                whole((18, 64, 256)),
                whole((64, 432)),
                whole((64, 1728)),
                whole((1, 64)),
                whole((16, 64)),
            ],
            out_specs=[whole((64, 2, 16, 128)), whole((4, 8, 4, 16, 128))],
            scratch_shapes=[
                pltpu.VMEM((6 * 20 * 48, 128), BF),
                pltpu.VMEM((4 * 18 * 192, 128), BF),
                pltpu.VMEM((1024, 256), BF),
                pltpu.VMEM((128, 512), BF),
            ],
        ),
        out_shape=[
            jax.ShapeDtypeStruct((64, 2, 16, 128), BF),
            jax.ShapeDtypeStruct((4, 8, 4, 16, 128), BF),
        ],
        interpret=INTERPRET,
        name="coarse",
    )(at, got, near, far, w1, w2, b2, proj)


def shift(array, axis, by):
    count = lax.axis_size(axis)
    return lax.ppermute(array, axis, [(i, (i + by) % count) for i in range(count)])


def across_y(down, up, from_left, from_right):
    down = lax.dynamic_update_slice(down, jnp.concatenate([from_left[112:128], from_right[112:128]]), (1024, 0))
    up = lax.dynamic_update_slice(up, jnp.concatenate([from_left[0:16], from_right[0:16]]), (1024, 0))
    return shift(down, "wide", 1), shift(up, "wide", -1)


def turns(by):
    pairs = []
    for a in range(4):
        for b in range(8):
            to = (a + by * ((b == 7) - (b == 0))) % 4
            pairs += [((8 * a + b) * 4 + n, (8 * n + b) * 4 + to) for n in range(4)]
    return pairs


def taps(w):
    return jnp.transpose(w, (2, 3, 4, 0, 1)).reshape(27, w.shape[0], w.shape[1])


def local(
    fine_in,
    coarse_in,
    w_fine1,
    b_fine1,
    w_fine2,
    b_fine2,
    w_coarse1,
    b_coarse1,
    w_coarse2,
    b_coarse2,
    w_proj,
):
    w = lax.axis_index("wide")
    n = lax.axis_index("narrow")
    reaches = jnp.where(w % 2 == 1, w < 31, w > 0).astype(jnp.int32)
    at = jnp.stack([w // 8, w % 8, n, w, w % 2, reaches])
    rows, down, up, cols = prep(fine_in)
    ct, east, west = cprep(coarse_in, cols)
    from_left = shift(east, "narrow", 1)
    from_right = shift(west, "narrow", -1)
    top, bottom = across_y(down, up, from_left, from_right)
    wf1, wf2, wa, wb, wc = weights(taps(w_fine1), taps(w_fine2), taps(w_coarse1), taps(w_coarse2))
    slab = jnp.concatenate(
        [
            jnp.where(n > 0, from_left[128:], jnp.zeros((), BF)).reshape(2, 2, 64, 128),
            ct,
            jnp.where(n < 3, from_right[128:], jnp.zeros((), BF)).reshape(2, 2, 64, 128),
        ],
        axis=1,
    )
    mate = lax.ppermute(slab, "wide", [(i, i ^ 1) for i in range(32)])
    hops = [(i, i + 2 - 4 * (i % 2)) for i in range(32)]
    far = lax.ppermute(mate, "wide", [(i, j % 32) for i, j in hops])
    hidden, pooled, hcols, hdown, hup = fine1(
        at, rows, top, bottom, from_left, from_right, wf1, b_fine1[None]
    )
    turned = lax.ppermute(pooled, ("wide", "narrow"), turns(0))
    ends = lax.ppermute(pooled, ("wide", "narrow"), turns(1))
    slabs = jnp.stack([turned, ends]).reshape(2, 32, 16, 128)
    slabs = jnp.pad(slabs, ((0, 0), (1, 1), (0, 0), (0, 0)))
    parcels = jnp.stack([slabs[:, j : j + 32] for j in range(3)], axis=2).transpose(1, 0, 2, 3, 4)
    got = lax.all_to_all(parcels.reshape(32, 96, 128), "wide", 0, 0, tiled=True)
    near_part = conv1a(at, slab, mate, wa, b_coarse1[None], "near")
    hleft = shift(hcols, "narrow", 1)
    hright = shift(hcols, "narrow", -1)
    htop, hbottom = across_y(hdown, hup, hleft, hright)
    far_part = conv1a(at, far, slab, wa, b_coarse1[None], "distant")
    coarse_out, context = coarse(at, got.reshape(32, 2, 48, 128), near_part, far_part, wb, wc, b_coarse2[None], w_proj)
    arrived = lax.all_to_all(context.reshape(128, 16, 128), ("wide", "narrow"), 0, 0, tiled=True)
    term = fine2(at, hidden, htop, hbottom, hleft, hright, wf2, b_fine2[None])
    fine_out = final(at, term, arrived.reshape(32, 4, 16, 128))
    return fine_out, coarse_out


def solution(mesh):
    return jax.shard_map(
        local,
        mesh=mesh,
        in_specs=(P(None, None, "wide", "narrow"), P(None, "wide", "narrow", None)) + (P(),) * 9,
        out_specs=(P(None, None, "wide", "narrow"), P(None, "wide", "narrow", None)),
        check_vma=False,
    )
```

```python
import functools

import jax
import jax.numpy as jnp
from jax import lax
from jax.experimental import pallas as pl
from jax.experimental.pallas import tpu as pltpu
from jax.sharding import PartitionSpec as P


BF = jnp.bfloat16
F32 = jnp.float32
TERM = jnp.bfloat16
INTERPRET = False


def iota(shape, axis):
    return lax.broadcasted_iota(jnp.int32, shape, axis)


def onehot(mask):
    return jnp.where(mask, 1.0, 0.0).astype(BF)


def mm(a, b):
    return jnp.dot(a, b, preferred_element_type=F32)


def vm(n):
    return [pl.BlockSpec(memory_space=pltpu.VMEM)] * n


def outer_columns(rows, first_z):
    shape = (rows.shape[1], 128)
    r, lane = iota(shape, 0), iota(shape, 1)
    z, x = first_z + r // 128, r % 128
    return mm(rows, onehot(((x == 0) & (lane == z)) | ((x == 127) & (lane == z + 64))))


def prep_body(x_ref, t_ref, down_ref, up_ref, cols_ref, acc_ref):
    step = pl.program_id(0)
    zb = t_ref.shape[0]
    r, k = iota((128, 128), 0), iota((128, 128), 1)
    perm = onehot((r % 16) * 8 + r // 16 == k)
    rows = []
    for i in range(0, zb, 2):
        pair = jnp.concatenate([x_ref[:, step * zb + i + j].reshape(128, 128) for j in range(2)], axis=1)
        out = mm(perm, pair).astype(BF)
        for j in range(2):
            v = out[:, j * 128 : j * 128 + 128]
            t_ref[i + j] = v
            down_ref[(i + j) * 16 : (i + j) * 16 + 16, :] = v[112:128]
            up_ref[(i + j) * 16 : (i + j) * 16 + 16, :] = v[0:16]
        rows.append(out)
    part = outer_columns(jnp.concatenate(rows, axis=1), step * zb)

    @pl.when(step == 0)
    def _():
        acc_ref[...] = part

    @pl.when(step > 0)
    def _():
        acc_ref[...] += part

    cols_ref[...] = acc_ref[...].astype(BF)


def prep(x):
    zb = 8
    return pl.pallas_call(
        prep_body,
        grid=(64 // zb,),
        in_specs=[pl.BlockSpec((16, 64, 8, 128), lambda i: (0, 0, 0, 0))],
        out_specs=[
            pl.BlockSpec((zb, 128, 128), lambda i: (i, 0, 0)),
            pl.BlockSpec((zb * 16, 128), lambda i: (i, 0)),
            pl.BlockSpec((zb * 16, 128), lambda i: (i, 0)),
            pl.BlockSpec((128, 128), lambda i: (0, 0)),
        ],
        out_shape=[
            jax.ShapeDtypeStruct((64, 128, 128), BF),
            jax.ShapeDtypeStruct((1056, 128), BF),
            jax.ShapeDtypeStruct((1056, 128), BF),
            jax.ShapeDtypeStruct((128, 128), BF),
        ],
        scratch_shapes=[pltpu.VMEM((128, 128), F32)],
        interpret=INTERPRET,
        name="prep",
    )(x)


def cprep_body(x_ref, o_ref, east_ref, west_ref):
    r, k = iota((256, 256), 0), iota((256, 256), 1)
    perm = onehot((r % 16) * 16 + r // 16 == k)
    for g in range(4):
        pair = jnp.concatenate(
            [x_ref[g * 16 : g * 16 + 16, z].reshape(256, 128) for z in range(2)], axis=1
        )
        out = mm(perm, pair).astype(BF)
        for z in range(2):
            for y in range(16):
                v = out[y * 16 : y * 16 + 16, z * 128 : z * 128 + 128]
                o_ref[z, y, g * 16 : g * 16 + 16, :] = v
                row = z * 128 + (y % 2) * 64 + g * 16
                if y >= 14:
                    east_ref[row : row + 16, :] = v
                if y < 2:
                    west_ref[row : row + 16, :] = v


def cprep(x):
    return pl.pallas_call(
        cprep_body,
        in_specs=vm(1),
        out_specs=vm(3),
        out_shape=[
            jax.ShapeDtypeStruct((2, 16, 64, 128), BF),
            jax.ShapeDtypeStruct((256, 128), BF),
            jax.ShapeDtypeStruct((256, 128), BF),
        ],
        interpret=INTERPRET,
        name="cprep",
    )(x)


def weights_body(f1_ref, f2_ref, c1_ref, c2_ref, wf1_ref, wf2_ref, wa_ref, wb_ref, wc_ref, w0_ref):
    for k_ref, w_ref in ((f1_ref, wf1_ref), (f2_ref, wf2_ref)):
        w0_ref[...] = jnp.zeros((16, 1536), F32)
        for t in range(27):
            dz, dy, dx = t // 9, t // 3 % 3, t % 3
            at = dz * 512 + dx * 160 + dy * 16
            w0_ref[:, at : at + 16] = k_ref[t].astype(F32)
        w0 = w0_ref[...]
        for y in range(8):
            w_ref[y * 16 : y * 16 + 16, :] = (pltpu.roll(w0, y * 16, 1) if y else w0).astype(BF)
    r, k = iota((128, 128), 0), iota((128, 128), 1)
    wf2_ref[...] = mm(onehot((r % 8) * 16 + r // 8 == k), wf2_ref[...]).astype(BF)
    for t in range(27):
        both = c1_ref[t]
        wa_ref[:, t * 64 : t * 64 + 64] = both[:, 0:64]
        wb_ref[:, t * 16 : t * 16 + 16] = both[:, 64:80]
        wc_ref[:, t * 64 : t * 64 + 64] = c2_ref[t]


def weights(f1, f2, c1, c2):
    return pl.pallas_call(
        weights_body,
        in_specs=vm(4),
        out_specs=vm(5),
        out_shape=[
            jax.ShapeDtypeStruct((128, 1536), BF),
            jax.ShapeDtypeStruct((128, 1536), BF),
            jax.ShapeDtypeStruct((64, 1728), BF),
            jax.ShapeDtypeStruct((64, 432), BF),
            jax.ShapeDtypeStruct((64, 1728), BF),
        ],
        scratch_shapes=[pltpu.VMEM((16, 1536), F32)],
        interpret=INTERPRET,
        name="weights",
    )(f1, f2, c1, c2)


def kept(ok, v):
    return jnp.where(ok, v, jnp.zeros((), BF))


def stage(z, at_ref, x_ref, top_ref, bot_ref, tl_ref, tr_ref, s_ref):
    rows = pl.ds(pl.multiple_of(z * 16, 16), 16)
    top = kept(at_ref[3] > 0, top_ref[rows, :])
    bot = kept(at_ref[3] < 31, bot_ref[rows, :])
    v = jnp.concatenate([top, x_ref[z], bot], axis=0)
    lane = iota((160, 128), 1)
    left = jnp.where(lane == 0, pltpu.roll(tl_ref[...], lax.rem(192 - z, 128), 1), pltpu.roll(v, 1, 1))
    right = jnp.where(lane == 127, pltpu.roll(tr_ref[...], 127 - z, 1), pltpu.roll(v, 127, 1))
    base = pl.multiple_of((z + 1) * 512, 512)
    s_ref[pl.ds(base, 160), :] = left
    s_ref[pl.ds(base + 160, 160), :] = v
    s_ref[pl.ds(base + 320, 160), :] = right


def conv_pair(z, w_ref, s_ref):
    base = pl.multiple_of(z * 512, 512)
    rhs = jnp.concatenate([s_ref[pl.ds(base, 1536), :], s_ref[pl.ds(base + 512, 1536), :]], axis=1)
    return mm(w_ref[...], rhs)


def bias_rows(b_ref, count, row_of):
    shape = (count, b_ref.shape[1])
    r, k = iota(shape, 0), iota(shape, 1)
    return jnp.sum(jnp.where(row_of(r) == k, b_ref[...], 0.0), axis=1, keepdims=True)


def fine_setup(at_ref, top_ref, bot_ref, cl_ref, cr_ref, s_ref, tl_ref, tr_ref):
    n, w = at_ref[2], at_ref[3]
    for ref, edge, col, ok in ((tl_ref, 1024, cl_ref, n > 0), (tr_ref, 1040, cr_ref, n < 3)):
        ref[0:16, :] = kept(ok & (w > 0), top_ref[edge : edge + 16, :])
        ref[16:144, :] = kept(ok, col[0:128, :])
        ref[144:160, :] = kept(ok & (w < 31), bot_ref[edge : edge + 16, :])
    s_ref[0:512, :] = jnp.zeros((512, 128), BF)
    s_ref[65 * 512 : 66 * 512, :] = jnp.zeros((512, 128), BF)
    for z in range(1, 65):
        s_ref[z * 512 + 480 : z * 512 + 512, :] = jnp.zeros((32, 128), BF)


def run_conv(stage_fn, finish, w_ref, s_ref):
    for z in range(5):
        stage_fn(z)

    def step(i, _):
        first = conv_pair(4 * i, w_ref, s_ref)
        second = conv_pair(4 * i + 2, w_ref, s_ref)
        for k in range(5, 9):
            stage_fn(4 * i + k)
        finish(2 * i, first)
        finish(2 * i + 1, second)
        return 0

    lax.fori_loop(0, 14, step, 0)
    first = conv_pair(56, w_ref, s_ref)
    second = conv_pair(58, w_ref, s_ref)
    for k in range(61, 64):
        stage_fn(k)
    finish(28, first)
    finish(29, second)
    first = conv_pair(60, w_ref, s_ref)
    second = conv_pair(62, w_ref, s_ref)
    finish(30, first)
    finish(31, second)


def fine1_body(at_ref, x_ref, top_ref, bot_ref, cl_ref, cr_ref, w_ref, b_ref, h_ref, p_ref, cols_ref, down_ref, up_ref, s_ref, tl_ref, tr_ref, acc_ref):
    fine_setup(at_ref, top_ref, bot_ref, cl_ref, cr_ref, s_ref, tl_ref, tr_ref)
    bias = bias_rows(b_ref, 128, lambda r: r % 16)

    def finish(i, out):
        h = jnp.maximum(out + bias, 0.0).astype(BF)
        parts = []
        for k in range(2):
            hz = h[:, k * 128 : (k + 1) * 128]
            h_ref[2 * i + k] = hz
            row = pl.ds(pl.multiple_of((2 * i + k) * 16, 16), 16)
            down_ref[row, :] = hz[112:128]
            up_ref[row, :] = hz[0:16]
            f = hz.astype(F32)
            for half in range(2):
                r = f[half * 64 : half * 64 + 64]
                parts.append((r[0:16] + r[16:32]) + (r[32:48] + r[48:64]))
        hi = [p.astype(BF) for p in parts]
        lo = [(p - q.astype(F32)).astype(BF) for p, q in zip(parts, hi)]
        acc_ref[pl.ds(pl.multiple_of(i * 16, 16), 16), :] = jnp.concatenate(hi + lo, axis=1)

    run_conv(lambda z: stage(z, at_ref, x_ref, top_ref, bot_ref, tl_ref, tr_ref, s_ref), finish, w_ref, s_ref)
    r, lane = iota((1024, 128), 0) % 512, iota((1024, 128), 1)
    pick = jnp.where((r // 128) * 32 + (r % 128) // 4 == lane, 0.0625, 0.0).astype(BF)
    p_ref[...] = mm(acc_ref[...], pick).astype(BF)
    total = jnp.zeros((128, 128), F32)
    for g in range(8):
        total = total + outer_columns(jnp.concatenate([h_ref[g * 8 + k] for k in range(8)], axis=1), g * 8)
    cols_ref[...] = total.astype(BF)


def fine_scratch():
    return [
        pltpu.VMEM((66 * 512, 128), BF),
        pltpu.VMEM((160, 128), BF),
        pltpu.VMEM((160, 128), BF),
    ]


def fine1(at, x, top, bot, cl, cr, w, b):
    return pl.pallas_call(
        fine1_body,
        in_specs=[pl.BlockSpec(memory_space=pltpu.SMEM)] + vm(7),
        out_specs=vm(5),
        out_shape=[
            jax.ShapeDtypeStruct((64, 128, 128), BF),
            jax.ShapeDtypeStruct((512, 128), BF),
            jax.ShapeDtypeStruct((128, 128), BF),
            jax.ShapeDtypeStruct((1056, 128), BF),
            jax.ShapeDtypeStruct((1056, 128), BF),
        ],
        scratch_shapes=fine_scratch() + [pltpu.VMEM((512, 1024), BF)],
        interpret=INTERPRET,
        name="fine1",
    )(at, x, top, bot, cl, cr, w, b)


def fine2_body(at_ref, x_ref, top_ref, bot_ref, cl_ref, cr_ref, w_ref, b_ref, o_ref, s_ref, tl_ref, tr_ref):
    fine_setup(at_ref, top_ref, bot_ref, cl_ref, cr_ref, s_ref, tl_ref, tr_ref)
    bias = bias_rows(b_ref, 128, lambda r: r // 8)

    def finish(i, out):
        v = (out + bias).astype(TERM)
        for k in range(2):
            o_ref[2 * i + k] = v[:, k * 128 : (k + 1) * 128]

    run_conv(lambda z: stage(z, at_ref, x_ref, top_ref, bot_ref, tl_ref, tr_ref, s_ref), finish, w_ref, s_ref)


def fine2(at, x, top, bot, cl, cr, w, b):
    return pl.pallas_call(
        fine2_body,
        in_specs=[pl.BlockSpec(memory_space=pltpu.SMEM)] + vm(7),
        out_specs=vm(1)[0],
        out_shape=jax.ShapeDtypeStruct((64, 128, 128), TERM),
        scratch_shapes=fine_scratch(),
        interpret=INTERPRET,
        name="fine2",
    )(at, x, top, bot, cl, cr, w, b)


def final_body(at_ref, t_ref, c_ref, o_ref):
    r, lane = iota((128, 512), 0), iota((128, 512), 1)
    up = onehot((lane // 128) * 32 + (lane % 128) // 4 == r)
    e = mm(c_ref[...].reshape(128, 128), up).astype(BF)
    rr, kk = iota((128, 32), 0), iota((128, 32), 1)
    widen = onehot((kk % 16 == rr // 8) & (kk // 16 == (rr % 8) // 4))
    both = []
    for p in range(8):
        row = e[p * 16 : p * 16 + 16]
        for k in range(2):
            both.append(
                jnp.concatenate([row[:, k * 256 : k * 256 + 128], row[:, k * 256 + 128 : k * 256 + 256]], axis=0)
            )
    c = mm(widen, jnp.concatenate(both, axis=1))
    for z in range(16):
        v = t_ref[z].astype(F32) + c[:, z * 128 : z * 128 + 128]
        o_ref[:, z] = v.reshape(16, 8, 128).astype(BF)


def final(at, t, c):
    return pl.pallas_call(
        final_body,
        grid_spec=pltpu.PrefetchScalarGridSpec(
            num_scalar_prefetch=1,
            grid=(4,),
            in_specs=[
                pl.BlockSpec((16, 128, 128), lambda i, at: (i, 0, 0)),
                pl.BlockSpec((8, 1, 16, 128), lambda i, at: (i, at[0], 0, 0)),
            ],
            out_specs=pl.BlockSpec((16, 16, 8, 128), lambda i, at: (0, i, 0, 0)),
        ),
        out_shape=jax.ShapeDtypeStruct((16, 64, 8, 128), BF),
        interpret=INTERPRET,
        name="final",
    )(at, t, c)


def spread_x(v):
    lane = iota(v.shape, 1)
    left = jnp.where(lane == 0, jnp.zeros((), BF), pltpu.roll(v, 1, 1))
    right = jnp.where(lane == 127, jnp.zeros((), BF), pltpu.roll(v, 127, 1))
    return jnp.concatenate([left, v, right], axis=0)


def window(s_ref, z, y, rows, per_z):
    both = []
    for k in range(2):
        parts = [
            s_ref[pl.ds(pl.multiple_of((z + dz) * per_z + (y + k) * rows, 16), 3 * rows), :] for dz in range(3)
        ]
        both.append(jnp.concatenate(parts, axis=0))
    return jnp.concatenate(both, axis=1)


def conv1a_body(masked, at_ref, first_ref, second_ref, w_ref, b_ref, o_ref, s_ref):
    swap = at_ref[4] == 1
    reaches = at_ref[5] == 1

    def fill(y, _):
        for zi in range(2):
            a, b = first_ref[zi, y], second_ref[zi, y]
            if masked:
                a = kept(reaches, a)
            for at, v in ((zi, jnp.where(swap, b, a)), (zi + 2, jnp.where(swap, a, b))):
                s_ref[pl.ds(pl.multiple_of(at * 3840 + y * 192, 64), 192), :] = spread_x(v)
        return 0

    lax.fori_loop(0, 20, fill, 0)
    bias = bias_rows(b_ref, 64, lambda r: r)

    def step(i, _):
        outs = [
            mm(w_ref[...], window(s_ref, zo, 6 * i + 2 * k, 192, 3840)) + bias for zo in range(2) for k in range(3)
        ]
        for j in range(6):
            o_ref[j // 3 * 9 + 3 * i + j % 3] = outs[j]
        return 0

    lax.fori_loop(0, 3, step, 0)


def conv1a(at, first, second, w, b, name):
    return pl.pallas_call(
        functools.partial(conv1a_body, name == "distant"),
        in_specs=[pl.BlockSpec(memory_space=pltpu.SMEM)] + vm(4),
        out_specs=vm(1)[0],
        out_shape=jax.ShapeDtypeStruct((18, 64, 256), F32),
        scratch_shapes=[pltpu.VMEM((4 * 20 * 192, 128), BF)],
        interpret=INTERPRET,
    )(at, first, second, w, b)


def coarse_body(at_ref, got_ref, near_ref, far_ref, w1_ref, w2_ref, b_ref, proj_ref, out_ref, ctx_ref, sp_ref, sm_ref, co_ref, ct_ref):
    n, w = at_ref[2], at_ref[3]
    odd = at_ref[4] == 1
    r, c = iota((512, 512), 0), iota((512, 512), 1)
    order = onehot((r % 128 // 32 == c // 128) & (r // 128 == c % 128 // 32) & (r % 32 == c % 32))
    for wb in range(10):
        if wb == 0:
            blocks = [kept(n > 0, got_ref[8 * k + 7, 1]) for k in range(4)]
        elif wb == 9:
            blocks = [kept(n < 3, got_ref[8 * k, 1]) for k in range(4)]
        else:
            blocks = [got_ref[8 * k + wb - 1, 0] for k in range(4)]
        t = mm(jnp.concatenate(blocks, axis=1), order).astype(BF)
        for s in range(3):
            for zi in range(4):
                v = t[s * 16 : s * 16 + 16, zi * 128 : zi * 128 + 128]
                base = (2 * s + zi // 2) * 960 + (2 * wb + zi % 2) * 48
                sp_ref[base : base + 48, :] = spread_x(v)

    def mid(yp, _):
        outs = []
        for zo in range(4):
            i = zo % 2 * 9 + yp
            low, high = (far_ref, near_ref) if zo < 2 else (near_ref, far_ref)
            part = jnp.where(odd, high[i], low[i])
            outs.append(mm(w1_ref[...], window(sp_ref, zo, 2 * yp, 48, 960)) + part)
        keep = [(yp > 0) | (n > 0), (yp < 8) | (n < 3)]
        for zo in range(4):
            v = jnp.maximum(outs[zo], 0.0)
            for k in range(2):
                inside = keep[k] & (w > 0) if zo == 0 else keep[k] & (w < 31) if zo == 3 else keep[k]
                m = jnp.where(inside, v[:, k * 128 : k * 128 + 128], 0.0).astype(BF)
                sm_ref[pl.ds(pl.multiple_of(zo * 3456 + (2 * yp + k) * 192, 64), 192), :] = spread_x(m)
        return 0

    lax.fori_loop(0, 9, mid, 0)
    bias = bias_rows(b_ref, 64, lambda r: r)
    proj = proj_ref[...]

    def last(i, _):
        outs = [mm(w2_ref[...], window(sm_ref, z, 4 * i + 2 * h, 192, 3456)) for z in range(2) for h in range(2)]
        for j in range(4):
            z, b = j // 2, 2 * i + j % 2
            o = jnp.maximum(outs[j] + bias, 0.0).astype(BF)
            ct = mm(proj, o).astype(BF)
            for k in range(2):
                lanes = slice(k * 128, k * 128 + 128)
                co_ref[pl.ds(pl.multiple_of((2 * b + k) * 64, 64), 64), z * 128 : z * 128 + 128] = o[:, lanes]
                at = (z * 2 + k) * 128
                ct_ref[pl.ds(pl.multiple_of(b * 16, 16), 16), at : at + 128] = ct[:, lanes]
        return 0

    lax.fori_loop(0, 4, last, 0)
    back = onehot((c % 128 // 32 == r // 128) & (c // 128 == r % 128 // 32) & (r % 32 == c % 32))
    ct = mm(ct_ref[...], back).astype(BF)
    for b in range(8):
        for k in range(4):
            block = ct[b * 16 : b * 16 + 16, k * 128 : k * 128 + 128]
            for to in range(4):
                ctx_ref[to, b, k] = jnp.where(n == to, block, jnp.zeros((), BF))
    r, k = iota((256, 256), 0), iota((256, 256), 1)
    perm = onehot((r % 16) * 16 + r // 16 == k)
    for g in range(4):
        rows = jnp.concatenate([co_ref[y * 64 + g * 16 : y * 64 + g * 16 + 16, :] for y in range(16)], axis=0)
        o = mm(perm, rows).astype(BF)
        for z in range(2):
            out_ref[g * 16 : g * 16 + 16, z] = o[:, z * 128 : z * 128 + 128].reshape(16, 16, 128)


def coarse(at, got, near, far, w1, w2, b2, proj):
    def whole(shape):
        return pl.BlockSpec(shape, lambda i, at: (0,) * len(shape))

    return pl.pallas_call(
        coarse_body,
        grid_spec=pltpu.PrefetchScalarGridSpec(
            num_scalar_prefetch=1,
            grid=(1,),
            in_specs=[
                whole((32, 2, 48, 128)),
                whole((18, 64, 256)),
                whole((18, 64, 256)),
                whole((64, 432)),
                whole((64, 1728)),
                whole((1, 64)),
                whole((16, 64)),
            ],
            out_specs=[whole((64, 2, 16, 128)), whole((4, 8, 4, 16, 128))],
            scratch_shapes=[
                pltpu.VMEM((6 * 20 * 48, 128), BF),
                pltpu.VMEM((4 * 18 * 192, 128), BF),
                pltpu.VMEM((1024, 256), BF),
                pltpu.VMEM((128, 512), BF),
            ],
        ),
        out_shape=[
            jax.ShapeDtypeStruct((64, 2, 16, 128), BF),
            jax.ShapeDtypeStruct((4, 8, 4, 16, 128), BF),
        ],
        interpret=INTERPRET,
        name="coarse",
    )(at, got, near, far, w1, w2, b2, proj)


def shift(array, axis, by):
    count = lax.axis_size(axis)
    return lax.ppermute(array, axis, [(i, (i + by) % count) for i in range(count)])


def across_y(down, up, from_left, from_right):
    down = lax.dynamic_update_slice(down, jnp.concatenate([from_left[112:128], from_right[112:128]]), (1024, 0))
    up = lax.dynamic_update_slice(up, jnp.concatenate([from_left[0:16], from_right[0:16]]), (1024, 0))
    return shift(down, "wide", 1), shift(up, "wide", -1)


def turns(by):
    pairs = []
    for a in range(4):
        for b in range(8):
            to = (a + by * ((b == 7) - (b == 0))) % 4
            pairs += [((8 * a + b) * 4 + n, (8 * n + b) * 4 + to) for n in range(4)]
    return pairs


def taps(w):
    return jnp.transpose(w, (2, 3, 4, 0, 1)).reshape(27, w.shape[0], w.shape[1])


def local(
    fine_in,
    coarse_in,
    w_fine1,
    b_fine1,
    w_fine2,
    b_fine2,
    w_coarse1,
    b_coarse1,
    w_coarse2,
    b_coarse2,
    w_proj,
):
    w = lax.axis_index("wide")
    n = lax.axis_index("narrow")
    reaches = jnp.where(w % 2 == 1, w < 31, w > 0).astype(jnp.int32)
    at = jnp.stack([w // 8, w % 8, n, w, w % 2, reaches])
    ct, east, west = cprep(coarse_in)
    before = shift(east, "narrow", 1)
    after = shift(west, "narrow", -1)
    slab = jnp.concatenate(
        [
            kept(n > 0, before).reshape(2, 2, 64, 128),
            ct,
            kept(n < 3, after).reshape(2, 2, 64, 128),
        ],
        axis=1,
    )
    mate = lax.ppermute(slab, "wide", [(i, i ^ 1) for i in range(32)])
    rows, down, up, cols = prep(fine_in)
    from_left = shift(cols, "narrow", 1)
    from_right = shift(cols, "narrow", -1)
    top, bottom = across_y(down, up, from_left, from_right)
    wf1, wf2, wa, wb, wc = weights(taps(w_fine1), taps(w_fine2), taps(w_coarse1), taps(w_coarse2))
    hops = [(i, i + 2 - 4 * (i % 2)) for i in range(32)]
    far = lax.ppermute(mate, "wide", [(i, j % 32) for i, j in hops])
    hidden, pooled, hcols, hdown, hup = fine1(
        at, rows, top, bottom, from_left, from_right, wf1, b_fine1[None]
    )
    turned = lax.ppermute(pooled, ("wide", "narrow"), turns(0))
    ends = lax.ppermute(pooled, ("wide", "narrow"), turns(1))
    slabs = jnp.stack([turned, ends]).reshape(2, 32, 16, 128)
    slabs = jnp.pad(slabs, ((0, 0), (1, 1), (0, 0), (0, 0)))
    parcels = jnp.stack([slabs[:, j : j + 32] for j in range(3)], axis=2).transpose(1, 0, 2, 3, 4)
    got = lax.all_to_all(parcels.reshape(32, 96, 128), "wide", 0, 0, tiled=True)
    near_part = conv1a(at, slab, mate, wa, b_coarse1[None], "near")
    hleft = shift(hcols, "narrow", 1)
    hright = shift(hcols, "narrow", -1)
    htop, hbottom = across_y(hdown, hup, hleft, hright)
    far_part = conv1a(at, far, slab, wa, b_coarse1[None], "distant")
    coarse_out, context = coarse(at, got.reshape(32, 2, 48, 128), near_part, far_part, wb, wc, b_coarse2[None], w_proj)
    arrived = lax.all_to_all(context.reshape(128, 16, 128), ("wide", "narrow"), 0, 0, tiled=True)
    term = fine2(at, hidden, htop, hbottom, hleft, hright, wf2, b_fine2[None])
    fine_out = final(at, term, arrived.reshape(32, 4, 16, 128))
    return fine_out, coarse_out


def solution(mesh):
    return jax.shard_map(
        local,
        mesh=mesh,
        in_specs=(P(None, None, "wide", "narrow"), P(None, "wide", "narrow", None)) + (P(),) * 9,
        out_specs=(P(None, None, "wide", "narrow"), P(None, "wide", "narrow", None)),
        check_vma=False,
    )
```

```python
import functools

import jax
import jax.numpy as jnp
from jax import lax
from jax.experimental import pallas as pl
from jax.experimental.pallas import tpu as pltpu
from jax.sharding import PartitionSpec as P


BF = jnp.bfloat16
F32 = jnp.float32
TERM = jnp.bfloat16
INTERPRET = False


def iota(shape, axis):
    return lax.broadcasted_iota(jnp.int32, shape, axis)


def onehot(mask):
    return jnp.where(mask, 1.0, 0.0).astype(BF)


def mm(a, b):
    return jnp.dot(a, b, preferred_element_type=F32)


def vm(n):
    return [pl.BlockSpec(memory_space=pltpu.VMEM)] * n


def outer_columns(rows, first_z):
    shape = (rows.shape[1], 128)
    r, lane = iota(shape, 0), iota(shape, 1)
    z, x = first_z + r // 128, r % 128
    return mm(rows, onehot(((x == 0) & (lane == z)) | ((x == 127) & (lane == z + 64))))


def prep_body(x_ref, t_ref, down_ref, up_ref, cols_ref, acc_ref):
    step = pl.program_id(0)
    zb = t_ref.shape[0]
    r, k = iota((128, 128), 0), iota((128, 128), 1)
    perm = onehot((r % 16) * 8 + r // 16 == k)
    rows = []
    for i in range(0, zb, 2):
        pair = jnp.concatenate([x_ref[:, step * zb + i + j].reshape(128, 128) for j in range(2)], axis=1)
        out = mm(perm, pair).astype(BF)
        for j in range(2):
            v = out[:, j * 128 : j * 128 + 128]
            t_ref[i + j] = v
            down_ref[(i + j) * 16 : (i + j) * 16 + 16, :] = v[112:128]
            up_ref[(i + j) * 16 : (i + j) * 16 + 16, :] = v[0:16]
        rows.append(out)
    part = outer_columns(jnp.concatenate(rows, axis=1), step * zb)

    @pl.when(step == 0)
    def _():
        acc_ref[...] = part

    @pl.when(step > 0)
    def _():
        acc_ref[...] += part

    cols_ref[...] = acc_ref[...].astype(BF)


def prep(x):
    zb = 8
    return pl.pallas_call(
        prep_body,
        grid=(64 // zb,),
        in_specs=[pl.BlockSpec((16, 64, 8, 128), lambda i: (0, 0, 0, 0))],
        out_specs=[
            pl.BlockSpec((zb, 128, 128), lambda i: (i, 0, 0)),
            pl.BlockSpec((zb * 16, 128), lambda i: (i, 0)),
            pl.BlockSpec((zb * 16, 128), lambda i: (i, 0)),
            pl.BlockSpec((128, 128), lambda i: (0, 0)),
        ],
        out_shape=[
            jax.ShapeDtypeStruct((64, 128, 128), BF),
            jax.ShapeDtypeStruct((1056, 128), BF),
            jax.ShapeDtypeStruct((1056, 128), BF),
            jax.ShapeDtypeStruct((128, 128), BF),
        ],
        scratch_shapes=[pltpu.VMEM((128, 128), F32)],
        interpret=INTERPRET,
        name="prep",
    )(x)


def cprep_body(x_ref, o_ref, east_ref, west_ref):
    r, k = iota((256, 256), 0), iota((256, 256), 1)
    perm = onehot((r % 16) * 16 + r // 16 == k)
    for g in range(4):
        pair = jnp.concatenate(
            [x_ref[g * 16 : g * 16 + 16, z].reshape(256, 128) for z in range(2)], axis=1
        )
        out = mm(perm, pair).astype(BF)
        for z in range(2):
            for y in range(16):
                v = out[y * 16 : y * 16 + 16, z * 128 : z * 128 + 128]
                o_ref[z, y, g * 16 : g * 16 + 16, :] = v
                row = z * 128 + (y % 2) * 64 + g * 16
                if y >= 14:
                    east_ref[row : row + 16, :] = v
                if y < 2:
                    west_ref[row : row + 16, :] = v


def cprep(x):
    return pl.pallas_call(
        cprep_body,
        in_specs=vm(1),
        out_specs=vm(3),
        out_shape=[
            jax.ShapeDtypeStruct((2, 16, 64, 128), BF),
            jax.ShapeDtypeStruct((256, 128), BF),
            jax.ShapeDtypeStruct((256, 128), BF),
        ],
        interpret=INTERPRET,
        name="cprep",
    )(x)


def weights_body(f1_ref, f2_ref, c1_ref, c2_ref, wf1_ref, wf2_ref, wa_ref, wb_ref, wc_ref, w0_ref):
    for k_ref, w_ref in ((f1_ref, wf1_ref), (f2_ref, wf2_ref)):
        w0_ref[...] = jnp.zeros((16, 1536), F32)
        for t in range(27):
            dz, dy, dx = t // 9, t // 3 % 3, t % 3
            at = dz * 512 + dx * 160 + dy * 16
            w0_ref[:, at : at + 16] = k_ref[t].astype(F32)
        w0 = w0_ref[...]
        for y in range(8):
            w_ref[y * 16 : y * 16 + 16, :] = (pltpu.roll(w0, y * 16, 1) if y else w0).astype(BF)
    r, k = iota((128, 128), 0), iota((128, 128), 1)
    wf2_ref[...] = mm(onehot((r % 8) * 16 + r // 8 == k), wf2_ref[...]).astype(BF)
    for t in range(27):
        both = c1_ref[t]
        wa_ref[:, t * 64 : t * 64 + 64] = both[:, 0:64]
        wb_ref[:, t * 16 : t * 16 + 16] = both[:, 64:80]
        wc_ref[:, t * 64 : t * 64 + 64] = c2_ref[t]


def weights(f1, f2, c1, c2):
    return pl.pallas_call(
        weights_body,
        in_specs=vm(4),
        out_specs=vm(5),
        out_shape=[
            jax.ShapeDtypeStruct((128, 1536), BF),
            jax.ShapeDtypeStruct((128, 1536), BF),
            jax.ShapeDtypeStruct((64, 1728), BF),
            jax.ShapeDtypeStruct((64, 432), BF),
            jax.ShapeDtypeStruct((64, 1728), BF),
        ],
        scratch_shapes=[pltpu.VMEM((16, 1536), F32)],
        interpret=INTERPRET,
        name="weights",
    )(f1, f2, c1, c2)


def kept(ok, v):
    return jnp.where(ok, v, jnp.zeros((), BF))


def stage(z, at_ref, x_ref, top_ref, bot_ref, tl_ref, tr_ref, s_ref):
    rows = pl.ds(pl.multiple_of(z * 16, 16), 16)
    top = kept(at_ref[3] > 0, top_ref[rows, :])
    bot = kept(at_ref[3] < 31, bot_ref[rows, :])
    v = jnp.concatenate([top, x_ref[z], bot], axis=0)
    lane = iota((160, 128), 1)
    left = jnp.where(lane == 0, pltpu.roll(tl_ref[...], lax.rem(192 - z, 128), 1), pltpu.roll(v, 1, 1))
    right = jnp.where(lane == 127, pltpu.roll(tr_ref[...], 127 - z, 1), pltpu.roll(v, 127, 1))
    base = pl.multiple_of((z + 1) * 512, 512)
    s_ref[pl.ds(base, 160), :] = left
    s_ref[pl.ds(base + 160, 160), :] = v
    s_ref[pl.ds(base + 320, 160), :] = right


def conv_pair(z, w_ref, s_ref):
    base = pl.multiple_of(z * 512, 512)
    rhs = jnp.concatenate([s_ref[pl.ds(base, 1536), :], s_ref[pl.ds(base + 512, 1536), :]], axis=1)
    return mm(w_ref[...], rhs)


def bias_rows(b_ref, count, row_of):
    shape = (count, b_ref.shape[1])
    r, k = iota(shape, 0), iota(shape, 1)
    return jnp.sum(jnp.where(row_of(r) == k, b_ref[...], 0.0), axis=1, keepdims=True)


def fine_setup(at_ref, top_ref, bot_ref, cl_ref, cr_ref, s_ref, tl_ref, tr_ref):
    n, w = at_ref[2], at_ref[3]
    for ref, edge, col, ok in ((tl_ref, 1024, cl_ref, n > 0), (tr_ref, 1040, cr_ref, n < 3)):
        ref[0:16, :] = kept(ok & (w > 0), top_ref[edge : edge + 16, :])
        ref[16:144, :] = kept(ok, col[0:128, :])
        ref[144:160, :] = kept(ok & (w < 31), bot_ref[edge : edge + 16, :])
    s_ref[0:512, :] = jnp.zeros((512, 128), BF)
    s_ref[65 * 512 : 66 * 512, :] = jnp.zeros((512, 128), BF)
    for z in range(1, 65):
        s_ref[z * 512 + 480 : z * 512 + 512, :] = jnp.zeros((32, 128), BF)


def run_conv(stage_fn, finish, w_ref, s_ref):
    for z in range(5):
        stage_fn(z)

    def step(i, _):
        first = conv_pair(4 * i, w_ref, s_ref)
        second = conv_pair(4 * i + 2, w_ref, s_ref)
        for k in range(5, 9):
            stage_fn(4 * i + k)
        finish(2 * i, first)
        finish(2 * i + 1, second)
        return 0

    lax.fori_loop(0, 14, step, 0)
    first = conv_pair(56, w_ref, s_ref)
    second = conv_pair(58, w_ref, s_ref)
    for k in range(61, 64):
        stage_fn(k)
    finish(28, first)
    finish(29, second)
    first = conv_pair(60, w_ref, s_ref)
    second = conv_pair(62, w_ref, s_ref)
    finish(30, first)
    finish(31, second)


def fine1_body(at_ref, x_ref, top_ref, bot_ref, cl_ref, cr_ref, w_ref, b_ref, h_ref, p_ref, cols_ref, down_ref, up_ref, s_ref, tl_ref, tr_ref, acc_ref):
    fine_setup(at_ref, top_ref, bot_ref, cl_ref, cr_ref, s_ref, tl_ref, tr_ref)
    bias = bias_rows(b_ref, 128, lambda r: r % 16)

    def finish(i, out):
        h = jnp.maximum(out + bias, 0.0).astype(BF)
        parts = []
        for k in range(2):
            hz = h[:, k * 128 : (k + 1) * 128]
            h_ref[2 * i + k] = hz
            row = pl.ds(pl.multiple_of((2 * i + k) * 16, 16), 16)
            down_ref[row, :] = hz[112:128]
            up_ref[row, :] = hz[0:16]
            f = hz.astype(F32)
            for half in range(2):
                r = f[half * 64 : half * 64 + 64]
                parts.append((r[0:16] + r[16:32]) + (r[32:48] + r[48:64]))
        hi = [p.astype(BF) for p in parts]
        lo = [(p - q.astype(F32)).astype(BF) for p, q in zip(parts, hi)]
        acc_ref[pl.ds(pl.multiple_of(i * 16, 16), 16), :] = jnp.concatenate(hi + lo, axis=1)

    run_conv(lambda z: stage(z, at_ref, x_ref, top_ref, bot_ref, tl_ref, tr_ref, s_ref), finish, w_ref, s_ref)
    r, lane = iota((1024, 128), 0) % 512, iota((1024, 128), 1)
    pick = jnp.where((r // 128) * 32 + (r % 128) // 4 == lane, 0.0625, 0.0).astype(BF)
    p_ref[...] = mm(acc_ref[...], pick).astype(BF)
    total = jnp.zeros((128, 128), F32)
    for g in range(8):
        total = total + outer_columns(jnp.concatenate([h_ref[g * 8 + k] for k in range(8)], axis=1), g * 8)
    cols_ref[...] = total.astype(BF)


def fine_scratch():
    return [
        pltpu.VMEM((66 * 512, 128), BF),
        pltpu.VMEM((160, 128), BF),
        pltpu.VMEM((160, 128), BF),
    ]


def fine1(at, x, top, bot, cl, cr, w, b):
    return pl.pallas_call(
        fine1_body,
        in_specs=[pl.BlockSpec(memory_space=pltpu.SMEM)] + vm(7),
        out_specs=vm(5),
        out_shape=[
            jax.ShapeDtypeStruct((64, 128, 128), BF),
            jax.ShapeDtypeStruct((512, 128), BF),
            jax.ShapeDtypeStruct((128, 128), BF),
            jax.ShapeDtypeStruct((1056, 128), BF),
            jax.ShapeDtypeStruct((1056, 128), BF),
        ],
        scratch_shapes=fine_scratch() + [pltpu.VMEM((512, 1024), BF)],
        interpret=INTERPRET,
        name="fine1",
    )(at, x, top, bot, cl, cr, w, b)


def fine2_body(at_ref, x_ref, top_ref, bot_ref, cl_ref, cr_ref, w_ref, b_ref, o_ref, s_ref, tl_ref, tr_ref):
    fine_setup(at_ref, top_ref, bot_ref, cl_ref, cr_ref, s_ref, tl_ref, tr_ref)
    bias = bias_rows(b_ref, 128, lambda r: r // 8)

    def finish(i, out):
        v = (out + bias).astype(TERM)
        for k in range(2):
            o_ref[2 * i + k] = v[:, k * 128 : (k + 1) * 128]

    run_conv(lambda z: stage(z, at_ref, x_ref, top_ref, bot_ref, tl_ref, tr_ref, s_ref), finish, w_ref, s_ref)


def fine2(at, x, top, bot, cl, cr, w, b):
    return pl.pallas_call(
        fine2_body,
        in_specs=[pl.BlockSpec(memory_space=pltpu.SMEM)] + vm(7),
        out_specs=vm(1)[0],
        out_shape=jax.ShapeDtypeStruct((64, 128, 128), TERM),
        scratch_shapes=fine_scratch(),
        interpret=INTERPRET,
        name="fine2",
    )(at, x, top, bot, cl, cr, w, b)


def final_body(at_ref, t_ref, c_ref, o_ref):
    r, lane = iota((128, 512), 0), iota((128, 512), 1)
    up = onehot((lane // 128) * 32 + (lane % 128) // 4 == r)
    e = mm(c_ref[...].reshape(128, 128), up).astype(BF)
    rr, kk = iota((128, 32), 0), iota((128, 32), 1)
    widen = onehot((kk % 16 == rr // 8) & (kk // 16 == (rr % 8) // 4))
    both = []
    for p in range(8):
        row = e[p * 16 : p * 16 + 16]
        for k in range(2):
            both.append(
                jnp.concatenate([row[:, k * 256 : k * 256 + 128], row[:, k * 256 + 128 : k * 256 + 256]], axis=0)
            )
    c = mm(widen, jnp.concatenate(both, axis=1))
    for z in range(16):
        v = t_ref[z].astype(F32) + c[:, z * 128 : z * 128 + 128]
        o_ref[:, z] = v.reshape(16, 8, 128).astype(BF)


def final(at, t, c):
    return pl.pallas_call(
        final_body,
        grid_spec=pltpu.PrefetchScalarGridSpec(
            num_scalar_prefetch=1,
            grid=(4,),
            in_specs=[
                pl.BlockSpec((16, 128, 128), lambda i, at: (i, 0, 0)),
                pl.BlockSpec((8, 1, 16, 128), lambda i, at: (i, at[0], 0, 0)),
            ],
            out_specs=pl.BlockSpec((16, 16, 8, 128), lambda i, at: (0, i, 0, 0)),
        ),
        out_shape=jax.ShapeDtypeStruct((16, 64, 8, 128), BF),
        interpret=INTERPRET,
        name="final",
    )(at, t, c)


def spread_x(v):
    lane = iota(v.shape, 1)
    left = jnp.where(lane == 0, jnp.zeros((), BF), pltpu.roll(v, 1, 1))
    right = jnp.where(lane == 127, jnp.zeros((), BF), pltpu.roll(v, 127, 1))
    return jnp.concatenate([left, v, right], axis=0)


def window(s_ref, z, y, rows, per_z):
    both = []
    for k in range(2):
        parts = [
            s_ref[pl.ds(pl.multiple_of((z + dz) * per_z + (y + k) * rows, 16), 3 * rows), :] for dz in range(3)
        ]
        both.append(jnp.concatenate(parts, axis=0))
    return jnp.concatenate(both, axis=1)


def conv1a_body(masked, at_ref, first_ref, second_ref, w_ref, b_ref, o_ref, s_ref):
    swap = at_ref[4] == 1
    reaches = at_ref[5] == 1

    def fill(y, _):
        for zi in range(2):
            a, b = first_ref[zi, y], second_ref[zi, y]
            if masked:
                a = kept(reaches, a)
            for at, v in ((zi, jnp.where(swap, b, a)), (zi + 2, jnp.where(swap, a, b))):
                s_ref[pl.ds(pl.multiple_of(at * 3840 + y * 192, 64), 192), :] = spread_x(v)
        return 0

    lax.fori_loop(0, 20, fill, 0)
    bias = bias_rows(b_ref, 64, lambda r: r)

    def step(i, _):
        outs = [
            mm(w_ref[...], window(s_ref, zo, 6 * i + 2 * k, 192, 3840)) + bias for zo in range(2) for k in range(3)
        ]
        for j in range(6):
            o_ref[j // 3 * 9 + 3 * i + j % 3] = outs[j]
        return 0

    lax.fori_loop(0, 3, step, 0)


def conv1a(at, first, second, w, b, name):
    return pl.pallas_call(
        functools.partial(conv1a_body, name == "distant"),
        in_specs=[pl.BlockSpec(memory_space=pltpu.SMEM)] + vm(4),
        out_specs=vm(1)[0],
        out_shape=jax.ShapeDtypeStruct((18, 64, 256), F32),
        scratch_shapes=[pltpu.VMEM((4 * 20 * 192, 128), BF)],
        interpret=INTERPRET,
    )(at, first, second, w, b)


def coarse_body(at_ref, got_ref, near_ref, far_ref, w1_ref, w2_ref, b_ref, proj_ref, out_ref, ctx_ref, sp_ref, sm_ref, co_ref, ct_ref):
    n, w = at_ref[2], at_ref[3]
    odd = at_ref[4] == 1
    r, c = iota((512, 512), 0), iota((512, 512), 1)
    order = onehot((r % 128 // 32 == c // 128) & (r // 128 == c % 128 // 32) & (r % 32 == c % 32))
    for wb in range(10):
        if wb == 0:
            blocks = [kept(n > 0, got_ref[8 * k + 7, 1]) for k in range(4)]
        elif wb == 9:
            blocks = [kept(n < 3, got_ref[8 * k, 1]) for k in range(4)]
        else:
            blocks = [got_ref[8 * k + wb - 1, 0] for k in range(4)]
        t = mm(jnp.concatenate(blocks, axis=1), order).astype(BF)
        for s in range(3):
            for zi in range(4):
                v = t[s * 16 : s * 16 + 16, zi * 128 : zi * 128 + 128]
                base = (2 * s + zi // 2) * 960 + (2 * wb + zi % 2) * 48
                sp_ref[base : base + 48, :] = spread_x(v)

    def mid(yp, _):
        outs = []
        for zo in range(4):
            i = zo % 2 * 9 + yp
            low, high = (far_ref, near_ref) if zo < 2 else (near_ref, far_ref)
            part = jnp.where(odd, high[i], low[i])
            outs.append(mm(w1_ref[...], window(sp_ref, zo, 2 * yp, 48, 960)) + part)
        keep = [(yp > 0) | (n > 0), (yp < 8) | (n < 3)]
        for zo in range(4):
            v = jnp.maximum(outs[zo], 0.0)
            for k in range(2):
                inside = keep[k] & (w > 0) if zo == 0 else keep[k] & (w < 31) if zo == 3 else keep[k]
                m = jnp.where(inside, v[:, k * 128 : k * 128 + 128], 0.0).astype(BF)
                sm_ref[pl.ds(pl.multiple_of(zo * 3456 + (2 * yp + k) * 192, 64), 192), :] = spread_x(m)
        return 0

    lax.fori_loop(0, 9, mid, 0)
    bias = bias_rows(b_ref, 64, lambda r: r)
    proj = proj_ref[...]

    def last(i, _):
        outs = [mm(w2_ref[...], window(sm_ref, z, 4 * i + 2 * h, 192, 3456)) for z in range(2) for h in range(2)]
        for j in range(4):
            z, b = j // 2, 2 * i + j % 2
            o = jnp.maximum(outs[j] + bias, 0.0).astype(BF)
            ct = mm(proj, o).astype(BF)
            for k in range(2):
                lanes = slice(k * 128, k * 128 + 128)
                co_ref[pl.ds(pl.multiple_of((2 * b + k) * 64, 64), 64), z * 128 : z * 128 + 128] = o[:, lanes]
                at = (z * 2 + k) * 128
                ct_ref[pl.ds(pl.multiple_of(b * 16, 16), 16), at : at + 128] = ct[:, lanes]
        return 0

    lax.fori_loop(0, 4, last, 0)
    back = onehot((c % 128 // 32 == r // 128) & (c // 128 == r % 128 // 32) & (r % 32 == c % 32))
    ct = mm(ct_ref[...], back).astype(BF)
    for b in range(8):
        for k in range(4):
            block = ct[b * 16 : b * 16 + 16, k * 128 : k * 128 + 128]
            for to in range(4):
                ctx_ref[to, b, k] = jnp.where(n == to, block, jnp.zeros((), BF))
    r, k = iota((256, 256), 0), iota((256, 256), 1)
    perm = onehot((r % 16) * 16 + r // 16 == k)
    for g in range(4):
        rows = jnp.concatenate([co_ref[y * 64 + g * 16 : y * 64 + g * 16 + 16, :] for y in range(16)], axis=0)
        o = mm(perm, rows).astype(BF)
        for z in range(2):
            out_ref[g * 16 : g * 16 + 16, z] = o[:, z * 128 : z * 128 + 128].reshape(16, 16, 128)


def coarse(at, got, near, far, w1, w2, b2, proj):
    def whole(shape):
        return pl.BlockSpec(shape, lambda i, at: (0,) * len(shape))

    return pl.pallas_call(
        coarse_body,
        grid_spec=pltpu.PrefetchScalarGridSpec(
            num_scalar_prefetch=1,
            grid=(1,),
            in_specs=[
                whole((32, 2, 48, 128)),
                whole((18, 64, 256)),
                whole((18, 64, 256)),
                whole((64, 432)),
                whole((64, 1728)),
                whole((1, 64)),
                whole((16, 64)),
            ],
            out_specs=[whole((64, 2, 16, 128)), whole((4, 8, 4, 16, 128))],
            scratch_shapes=[
                pltpu.VMEM((6 * 20 * 48, 128), BF),
                pltpu.VMEM((4 * 18 * 192, 128), BF),
                pltpu.VMEM((1024, 256), BF),
                pltpu.VMEM((128, 512), BF),
            ],
        ),
        out_shape=[
            jax.ShapeDtypeStruct((64, 2, 16, 128), BF),
            jax.ShapeDtypeStruct((4, 8, 4, 16, 128), BF),
        ],
        interpret=INTERPRET,
        name="coarse",
    )(at, got, near, far, w1, w2, b2, proj)


def shift(array, axis, by):
    count = lax.axis_size(axis)
    return lax.ppermute(array, axis, [(i, (i + by) % count) for i in range(count)])


def across_y(down, up, from_left, from_right):
    down = lax.dynamic_update_slice(down, jnp.concatenate([from_left[112:128], from_right[112:128]]), (1024, 0))
    up = lax.dynamic_update_slice(up, jnp.concatenate([from_left[0:16], from_right[0:16]]), (1024, 0))
    return shift(down, "wide", 1), shift(up, "wide", -1)


def turns(by):
    pairs = []
    for a in range(4):
        for b in range(8):
            to = (a + by * ((b == 7) - (b == 0))) % 4
            pairs += [((8 * a + b) * 4 + n, (8 * n + b) * 4 + to) for n in range(4)]
    return pairs


def taps(w):
    return jnp.transpose(w, (2, 3, 4, 0, 1)).reshape(27, w.shape[0], w.shape[1])


def local(
    fine_in,
    coarse_in,
    w_fine1,
    b_fine1,
    w_fine2,
    b_fine2,
    w_coarse1,
    b_coarse1,
    w_coarse2,
    b_coarse2,
    w_proj,
):
    w = lax.axis_index("wide")
    n = lax.axis_index("narrow")
    reaches = jnp.where(w % 2 == 1, w < 31, w > 0).astype(jnp.int32)
    at = jnp.stack([w // 8, w % 8, n, w, w % 2, reaches])
    ct, east, west = cprep(coarse_in)
    before = shift(east, "narrow", 1)
    after = shift(west, "narrow", -1)
    slab = jnp.concatenate(
        [
            kept(n > 0, before).reshape(2, 2, 64, 128),
            ct,
            kept(n < 3, after).reshape(2, 2, 64, 128),
        ],
        axis=1,
    )
    mate = lax.ppermute(slab, "wide", [(i, i ^ 1) for i in range(32)])
    rows, down, up, cols = prep(fine_in)
    from_left = shift(cols, "narrow", 1)
    from_right = shift(cols, "narrow", -1)
    top, bottom = across_y(down, up, from_left, from_right)
    wf1, wf2, wa, wb, wc = weights(taps(w_fine1), taps(w_fine2), taps(w_coarse1), taps(w_coarse2))
    hops = [(i, i + 2 - 4 * (i % 2)) for i in range(32)]
    far = lax.ppermute(mate, "wide", [(i, j % 32) for i, j in hops])
    hidden, pooled, hcols, hdown, hup = fine1(
        at, rows, top, bottom, from_left, from_right, wf1, b_fine1[None]
    )
    turned = lax.ppermute(pooled, ("wide", "narrow"), turns(0))
    ends = lax.ppermute(pooled, ("wide", "narrow"), turns(1))
    none = jnp.zeros((1, 16, 128), BF)
    slabs = [jnp.concatenate([none, tile.reshape(32, 16, 128), none]) for tile in (turned, ends)]
    parcels = jnp.concatenate([padded[j : j + 32] for padded in slabs for j in range(3)], axis=1)
    got = lax.all_to_all(parcels, "wide", 0, 0, tiled=True)
    near_part = conv1a(at, slab, mate, wa, b_coarse1[None], "near")
    hleft = shift(hcols, "narrow", 1)
    hright = shift(hcols, "narrow", -1)
    htop, hbottom = across_y(hdown, hup, hleft, hright)
    far_part = conv1a(at, far, slab, wa, b_coarse1[None], "distant")
    coarse_out, context = coarse(at, got.reshape(32, 2, 48, 128), near_part, far_part, wb, wc, b_coarse2[None], w_proj)
    arrived = lax.all_to_all(context.reshape(128, 16, 128), ("wide", "narrow"), 0, 0, tiled=True)
    term = fine2(at, hidden, htop, hbottom, hleft, hright, wf2, b_fine2[None])
    fine_out = final(at, term, arrived.reshape(32, 4, 16, 128))
    return fine_out, coarse_out


def solution(mesh):
    return jax.shard_map(
        local,
        mesh=mesh,
        in_specs=(P(None, None, "wide", "narrow"), P(None, "wide", "narrow", None)) + (P(),) * 9,
        out_specs=(P(None, None, "wide", "narrow"), P(None, "wide", "narrow", None)),
        check_vma=False,
    )
```
